128 devices in a mesh: frames: 2 (over y_hi), codebook: 16 (over y_lo, x, core), hidden: 4 (over z).
Axes of the slice: x: 4, y: 4 (y_hi: 2, y_lo: 2; y = y_hi * 2 + y_lo), z: 4, core: 2. Of those that a mesh axis runs over, the one named last changes fastest.
Arguments:
- temporal: bfloat16 [4096, 4096], P(('frames', 'codebook'), 'hidden'), may hold values from -6 to 6
- frame_ids: int32 [4096, 16], P('frames', 'codebook'), may hold values from 0 to 2047
- proj_weight: bfloat16 [16, 4096, 1024], P('codebook', 'hidden'), may hold values from -0.09375 to 0.09375
- embed_table: bfloat16 [16, 2049, 1024], P('codebook'), may hold values from -6 to 6
- qkv_weight: bfloat16 [16, 3, 1024, 1024], P('codebook', None, None, 'hidden'), may hold values from -12 to 12
- out_weight: bfloat16 [16, 1024, 1024], P('codebook', 'hidden'), may hold values from -0.1875 to 0.1875
- gate_up: bfloat16 [16, 2, 1024, 4096], P('codebook', None, None, 'hidden'), may hold values from -0.1875 to 0.1875
- down_weight: bfloat16 [16, 4096, 1024], P('codebook', 'hidden'), may hold values from -0.09375 to 0.09375
- norm_gains: float32 [16, 2, 1024], P('codebook'), may hold values from 0.25 to 1.75
Outputs:
- depth_states: float32 [16, 4096, 1024], P('codebook', 'frames', 'hidden')
The draws below stay inside these ranges and needn't reach their ends.
All inputs are finite; a program needn't handle non-finite values.
Results may differ from the reference program's by a relative error of at most 0.015.
Values may be sent and summed in bfloat16 or wider, within the bound.
A program may use at most 192 MiB of HBM per device.

```python
import math
import jax
import jax.numpy as jnp
from jax import lax

D = 4096
DD = 1024
HEADS = 16
HID = 4096
CARD = 2048
CODEBOOKS = 16
FRAMES = 4096


def draw_qkv_weight(key, part):
    base_key = jax.random.fold_in(key, 31)
    subkeys = jax.random.split(base_key, 5)
    base = jax.random.truncated_normal(subkeys[0], -4.0, 4.0, (CODEBOOKS, 3, DD, DD), jnp.float32) * DD ** (-0.5)
    chosen = jax.random.bernoulli(subkeys[1], 0.125, (CODEBOOKS, HEADS))
    first_book = jax.random.randint(subkeys[2], (), 0, CODEBOOKS)
    first_head = jax.random.randint(subkeys[3], (), 0, HEADS)
    forced = (jnp.arange(CODEBOOKS)[:, None] == first_book) & (jnp.arange(HEADS)[None, :] == first_head)
    chosen = chosen | forced
    lowest = 0.25
    spread = jax.random.uniform(subkeys[4], (CODEBOOKS, HEADS), jnp.float32, math.log(lowest), math.log(3.0))
    strength = jnp.exp(spread) * DD ** 0.5
    column_strength = jnp.repeat(strength, DD // HEADS, axis=1)
    column_chosen = jnp.repeat(chosen, DD // HEADS, axis=1)
    query_part = jnp.where(column_chosen[:, None, :], column_strength[:, None, :] * base[:, 1], base[:, 0])
    query_part = jnp.clip(query_part, -12.0, 12.0)
    return jnp.stack([query_part, base[:, 1], base[:, 2]], axis=1).astype(jnp.bfloat16)


def set_ends(entries, stream_key, least, largest):
    place = [jax.random.randint(jax.random.fold_in(stream_key, axis), (), 0, length) for axis, length in enumerate(entries.shape)]
    main_axis = entries.shape.index(max(entries.shape))
    next_to = place[:main_axis] + [(place[main_axis] + 1) % entries.shape[main_axis]] + place[main_axis + 1:]
    return entries.at[tuple(place)].set(least).at[tuple(next_to)].set(largest)


def block_scale(rng, extent, cuts, least, largest):
    loudness, own = 1.0, jax.random.fold_in(rng, 6)
    for axis_at, shards_of in cuts:
        steps = jnp.exp(jax.random.uniform(jax.random.fold_in(own, axis_at), (shards_of,), jnp.float32, least / len(cuts), largest / len(cuts)))
        loudness = loudness * jnp.repeat(steps, extent[axis_at] // shards_of).reshape([-1 if axis == axis_at else 1 for axis in range(len(extent))])
    return loudness


def noise(own_key, dims, scale, most, cuts=(), kind=jnp.bfloat16):
    values = scale * jax.random.normal(own_key, dims, jnp.float32)
    if cuts:
        values = values * block_scale(own_key, dims, cuts, -0.22, 0.18)
    return jnp.clip(values, -most, most).astype(kind)


def setup_inputs(seed: int = 0) -> dict:
    streams_of = jax.random.split(jax.random.key(seed), 10)
    return {
        "temporal": noise(streams_of[0], (FRAMES, D), 1.0, 6.0, ((0, 32), (1, 4))),
        "frame_ids": set_ends(jax.random.randint(streams_of[1], (FRAMES, CODEBOOKS), 0, CARD), jax.random.fold_in(streams_of[1], 1), 0, CARD - 1).astype(jnp.int32),
        "proj_weight": noise(streams_of[2], (CODEBOOKS, D, DD), D ** -0.5, 0.09375, ((0, 16), (1, 4))),
        "embed_table": noise(streams_of[3], (CODEBOOKS, CARD + 1, DD), 1.0, 6.0, ((0, 16),)),
        "qkv_weight": draw_qkv_weight(jax.random.fold_in(streams_of[9], 71), 0),
        "out_weight": noise(streams_of[5], (CODEBOOKS, DD, DD), DD ** -0.5, 0.1875, ((0, 16), (1, 4))),
        "gate_up": noise(streams_of[6], (CODEBOOKS, 2, DD, HID), DD ** -0.5, 0.1875, ((0, 16), (3, 4))),
        "down_weight": noise(streams_of[7], (CODEBOOKS, HID, DD), HID ** -0.5, 0.09375, ((0, 16), (1, 4))),
        "norm_gains": jnp.clip(1.0 + 0.15 * jax.random.normal(streams_of[8], (CODEBOOKS, 2, DD), jnp.float32), 0.25, 1.75),
    }


def normalize(values, gain):
    return values * lax.rsqrt(lax.optimization_barrier(jnp.mean(values * values, axis=-1, keepdims=True)) + 1e-05) * gain

def attend(queries, keys, values):
    positions = queries.shape[0]
    head_size = queries.shape[-1]
    scores = jnp.einsum('ifhd,jfhd->fhij', queries.astype(jnp.float32), keys.astype(jnp.float32)) * head_size ** (-0.5)
    causal = jnp.arange(positions)[:, None] >= jnp.arange(positions)[None, :]
    scores = jnp.where(causal, scores, -1e+30)
    highest = lax.optimization_barrier(jnp.max(scores, axis=-1, keepdims=True))
    weights = jnp.where(causal, jnp.exp(scores - highest), 0.0)
    running = lax.optimization_barrier(jnp.sum(weights, axis=-1))
    attended = jnp.einsum('fhij,jfhd->ifhd', weights.astype(jnp.bfloat16).astype(jnp.float32), values.astype(jnp.float32))
    return (attended / jnp.transpose(running, (2, 0, 1))[..., None]).astype(jnp.bfloat16)

def reference(temporal, frame_ids, proj_weight, embed_table, qkv_weight, out_weight, gate_up, down_weight, norm_gains):
    start_column = jnp.full((FRAMES, 1), CARD, jnp.int32)
    previous = jnp.concatenate([start_column, frame_ids[:, :-1].astype(jnp.int32)], axis=1)

    def first_half(inputs):
        projection, token_table, triple, norm_gain, token_ids = inputs
        x_zero = jnp.dot(temporal, projection, preferred_element_type=jnp.float32) + token_table[token_ids].astype(jnp.float32)
        normed = normalize(x_zero, norm_gain[0]).astype(jnp.bfloat16)
        outputs = [jnp.dot(normed, triple[i], preferred_element_type=jnp.float32).astype(jnp.bfloat16) for i in range(3)]
        return (x_zero, outputs[0], outputs[1], outputs[2])
    x_zero, queries, keys, values = lax.map(first_half, (proj_weight, embed_table, qkv_weight, norm_gains, previous.T))
    head_shape = (CODEBOOKS, FRAMES, HEADS, DD // HEADS)
    attended = attend(queries.reshape(head_shape), keys.reshape(head_shape), values.reshape(head_shape)).reshape(CODEBOOKS, FRAMES, DD)

    def second_half(inputs):
        base, attention, out_matrix, gate_pair, down_matrix, norm_gain = inputs
        residual = base + jnp.dot(attention, out_matrix, preferred_element_type=jnp.float32)
        normed = normalize(residual, norm_gain[1]).astype(jnp.bfloat16)
        gate_sum = jnp.dot(normed, gate_pair[0], preferred_element_type=jnp.float32)
        upper_sum = jnp.dot(normed, gate_pair[1], preferred_element_type=jnp.float32)
        activated = (jax.nn.silu(gate_sum) * upper_sum).astype(jnp.bfloat16)
        return residual + jnp.dot(activated, down_matrix, preferred_element_type=jnp.float32)
    return lax.map(second_half, (x_zero, attended, out_weight, gate_up, down_weight, norm_gains))
```

```python
import functools

import jax
import jax.numpy as jnp
from jax import lax
from jax.experimental import pallas as pl
from jax.experimental.pallas import tpu as pltpu
from jax.sharding import PartitionSpec as P

HEADS = 16
MESH = pl.DeviceIdType.MESH
F32 = jnp.float32
BF16 = jnp.bfloat16
CHIPS = ((0, 1), (0, 3), (1, 0), (0, 2), (1, 1), (1, 3), (1, 2))


def kernel(
    temporal, emb_in, wp_in, wqkv_in, wo_in, wgu_in, wd_in, gains, out,
    tbuf, wp, wqkv, wo, wgu, wd, emb,
    ps2, psr, psl, pfl, pfr, prl, prr, x0,
    n1, qs, qr, att_s, att_r, bias,
    n2, act, ds2, dsr, dsl, dfl, dfr, drl, drr, oacc,
    loc, t_s, t_r, wo_s, wo_r, p_s, p_r, n_s, n_r, m_s, m_r, a_s, a_r, b_s, b_r, d_s, d_r, o_s,
):
    f = lax.axis_index("frames")
    c = lax.axis_index("codebook")
    h = lax.axis_index("hidden")
    hr, hl, ho = (h + 1) % 4, (h + 3) % 4, (h + 2) % 4
    right, left = (f, c, hr), (f, c, hl)
    y, x, k = c // 8, (c // 2) % 4, c % 2
    order = (h, hl, hr, ho)

    def rc(src, dst, ss, rs, dev):
        return pltpu.make_async_remote_copy(
            src_ref=src, dst_ref=dst, send_sem=ss, recv_sem=rs, device_id=dev, device_id_type=MESH
        )

    def got(ref, ss, rs):
        rc(ref, ref, ss, rs, right).wait_recv()

    loads = [
        pltpu.make_async_copy(s, d, loc.at[i])
        for i, (s, d) in enumerate((
            (wp_in.at[0], wp), (wqkv_in.at[0], wqkv), (wgu_in.at[0], wgu), (wd_in.at[0], wd), (emb_in, emb),
            (wo_in.at[0], wo.at[h]), (temporal, tbuf.at[pl.ds(c * 128, 128)]),
        ))
    ]
    loads[6].start()
    loads[0].start()
    for i in (4, 1, 5, 2, 3):
        loads[i].start()

    barrier = pltpu.get_barrier_semaphore()

    def greet(n, carry):
        pl.semaphore_signal(
            barrier, inc=1, device_id=(f, (c + n // 4) % 16, (h + n % 4) % 4), device_id_type=MESH
        )
        return carry

    lax.fori_loop(1, 64, greet, 0)
    pl.semaphore_wait(barrier, 63)

    loads[6].wait()
    rows_of = lambda src: tbuf.at[pl.ds(src * 128, 128)]
    partner = (f, y * 8 + x * 2 + 1 - k, h)
    sends = []
    for i, (dy, dx) in enumerate(CHIPS):
        dst = ((y + dy) % 2) * 8 + ((x + dx) % 4) * 2 + k
        sends.append(rc(rows_of(c), rows_of(c), t_s.at[i], t_r.at[c], (f, dst, h)))
    sends.append(rc(rows_of(c), rows_of(c), t_s.at[7], t_r.at[c], partner))
    for s in sends:
        s.start()
    loads[5].wait()
    for j in (1, 3, 2):
        s = rc(wo.at[h], wo.at[h], wo_s.at[j - 1], wo_r.at[h], (f, c, (h + j) % 4))
        s.start()
        sends.append(s)
    for i, (dy, dx) in enumerate(CHIPS):
        src = ((y + 2 - dy) % 2) * 8 + ((x + 4 - dx) % 4) * 2 + k
        got(rows_of(src), t_s.at[0], t_r.at[src])
        s = rc(rows_of(src), rows_of(src), t_s.at[8 + i], t_r.at[src], partner)
        s.start()
        sends.append(s)
    for i, (dy, dx) in enumerate(((0, 0),) + CHIPS):
        src = ((y + dy) % 2) * 8 + ((x + dx) % 4) * 2 + 1 - k
        got(rows_of(src), t_s.at[0], t_r.at[src])
    loads[0].wait()

    def proj(block, row0, rows, store):
        def tile(n, carry):
            cols = pl.ds(pl.multiple_of(n * 256, 256), 256)
            lhs = tbuf[pl.ds(pl.multiple_of(block * 512 + row0, 256), rows), :]
            store(cols, jnp.dot(lhs, wp[:, cols], preferred_element_type=F32))
            return carry

        lax.fori_loop(0, 4, tile, 0)

    def into(ref, row0, rows, extra=None):
        def store(cols, value):
            if extra is not None:
                value = value + extra[:, cols].astype(F32)
            ref[pl.ds(row0, rows), cols] = value.astype(ref.dtype)

        return store

    top, bot = pl.ds(0, 256), pl.ds(256, 256)

    def send(src, dst, ss, rs, dev):
        s = rc(src, dst, ss, rs, dev)
        s.start()
        sends.append(s)

    proj(ho, 0, 512, into(ps2, 0, 512))
    send(ps2.at[top], pfl, p_s.at[0], p_r.at[0], right)
    send(ps2.at[bot], pfr, p_s.at[1], p_r.at[1], left)
    proj(hr, 256, 256, into(psr, 256, 256))
    send(psr.at[bot], prl.at[bot], p_s.at[2], p_r.at[2], right)
    proj(hl, 0, 256, into(psl, 0, 256))
    send(psl.at[top], prr.at[top], p_s.at[3], p_r.at[3], left)
    loads[4].wait()
    proj(h, 0, 512, into(x0, 0, 512, emb))
    got(pfl, p_s.at[0], p_r.at[0])
    proj(hr, 0, 256, into(psr, 0, 256, pfl))
    send(psr.at[top], prl.at[top], p_s.at[4], p_r.at[4], right)
    got(pfr, p_s.at[1], p_r.at[1])
    proj(hl, 256, 256, into(psl, 256, 256, pfr))
    send(psl.at[bot], prr.at[bot], p_s.at[5], p_r.at[5], left)
    for i, ref in ((2, prl.at[bot]), (3, prr.at[top]), (4, prl.at[top]), (5, prr.at[bot])):
        got(ref, p_s.at[i], p_r.at[i])

    def norm_rows(dst, gain, extras):
        def chunk(n, carry):
            rows = pl.ds(pl.multiple_of(n * 32, 32), 32)
            v = x0[rows, :]
            for e in extras:
                v = v + e[rows, :].astype(F32)
            if extras:
                x0[rows, :] = v
            scale = lax.rsqrt(jnp.mean(v * v, axis=-1, keepdims=True) + 1e-05)
            dst[h, rows, :] = (v * scale * gain).astype(BF16)
            return carry

        lax.fori_loop(0, 16, chunk, 0)

    norm_rows(n1, gains[0, 0:1, :], (prl, prr))

    def ag_start(buf, ss, rs):
        send(buf.at[h, top], buf.at[h, top], ss.at[0], rs.at[0], right)
        send(buf.at[h, bot], buf.at[h, bot], ss.at[2], rs.at[2], left)
        send(buf.at[h, bot], buf.at[h, bot], ss.at[1], rs.at[1], right)
        send(buf.at[h, top], buf.at[h, top], ss.at[3], rs.at[3], left)

    def ag_forward(buf, ss, rs):
        got(buf.at[hl, top], ss.at[0], rs.at[0])
        send(buf.at[hl, top], buf.at[hl, top], ss.at[4], rs.at[4], right)
        got(buf.at[hr, bot], ss.at[2], rs.at[2])
        send(buf.at[hr, bot], buf.at[hr, bot], ss.at[5], rs.at[5], left)

    def ag_wait(buf, ss, rs, pos):
        if pos == 1:
            got(buf.at[hl, bot], ss.at[1], rs.at[1])
        if pos == 2:
            got(buf.at[hr, top], ss.at[3], rs.at[3])
        if pos == 3:
            got(buf.at[ho, top], ss.at[4], rs.at[4])
            got(buf.at[ho, bot], ss.at[5], rs.at[5])

    ag_start(n1, n_s, n_r)

    row = lax.broadcasted_iota(jnp.int32, (256, 256), 0)
    col = lax.broadcasted_iota(jnp.int32, (256, 256), 1)
    seen = (row % 16 == col % 16) & (row // 16 >= col // 16)
    bias[...] = jnp.where(seen, 0.0, -1e30)
    loads[1].wait()

    def qkv(r):
        for i in range(3):
            part = jnp.dot(n1[r], wqkv[i], preferred_element_type=F32)
            qs[r, :, i * 256:(i + 1) * 256] = part.astype(BF16)

        def post(d, carry):
            dst = ((y + d // 8) % 2) * 8 + ((x + (d // 2) % 4) % 4) * 2 + (k + d) % 2
            rc(
                qs.at[r, pl.ds(dst * 32, 32)], qr.at[r, c], a_s.at[r, dst], a_r.at[r, c], (f, dst, h)
            ).start()
            return carry

        lax.fori_loop(1, 16, post, 0)
        qr[r, c] = qs[r, pl.ds(pl.multiple_of(c * 32, 32), 32), :]

    def attend(r):
        def arrived(d, carry):
            src = (c + d) % 16
            got(qr.at[r, src], a_s.at[r, 0], a_r.at[r, src])
            return carry

        lax.fori_loop(1, 16, arrived, 0)

        def unit(n, carry):
            frames = pl.ds(pl.multiple_of((n // 2) * 16, 16), 16)
            pair = (n % 2) * 128
            take = lambda i: qr[
                r, :, frames, pl.ds(pl.multiple_of(i * 256 + pair, 128), 128)
            ].reshape(256, 128)
            q, kk, v = take(0), take(1), take(2)
            lane = lax.broadcasted_iota(jnp.int32, (256, 128), 1)
            halves = []
            for half in range(2):
                mine = (lane // 64) == half
                qh = jnp.where(mine, q, jnp.zeros_like(q))
                parts = []
                for rows, width in ((slice(0, 128), 128), (slice(128, 256), 256)):
                    s = lax.dot_general(
                        qh[rows], kk[:width], (((1,), (1,)), ((), ())), preferred_element_type=F32
                    )
                    s = s * 0.125 + bias[rows, :width]
                    e = jnp.exp(s - jnp.max(s, axis=-1, keepdims=True))
                    total = jnp.sum(e, axis=-1, keepdims=True)
                    o = jnp.dot(e.astype(BF16), v[:width], preferred_element_type=F32)
                    parts.append(o / total)
                halves.append(jnp.concatenate(parts, axis=0))
            o = jnp.where((lane // 64) == 0, halves[0], halves[1]).astype(BF16)
            att_s[r, :, frames, pl.ds(pl.multiple_of(pair, 128), 128)] = o.reshape(16, 16, 128)
            return carry

        lax.fori_loop(0, 4, unit, 0)

        def post(d, carry):
            dst = ((y + d // 8) % 2) * 8 + ((x + (d // 2) % 4) % 4) * 2 + (k + d) % 2
            rc(
                att_s.at[r, dst], att_r.at[h, pl.ds(c * 32, 32)], b_s.at[r, dst], b_r.at[h, c], (f, dst, r)
            ).start()
            return carry

        return post

    def attend_own():
        lax.fori_loop(1, 16, attend(h), 0)
        att_r[h, pl.ds(pl.multiple_of(c * 32, 32), 32), :] = att_s[h, c]

    qkv(h)
    ag_forward(n1, n_s, n_r)
    attend_own()
    ag_wait(n1, n_s, n_r, 1)
    qkv(hl)
    ag_wait(n1, n_s, n_r, 2)
    qkv(hr)
    lax.fori_loop(0, 16, attend(hl), 0)
    lax.fori_loop(0, 16, attend(hr), 0)
    ag_wait(n1, n_s, n_r, 3)
    qkv(ho)
    lax.fori_loop(0, 16, attend(ho), 0)

    def out_part(src):
        def tile(n, carry):
            cols = pl.ds(pl.multiple_of(n * 256, 256), 256)
            x0[:, cols] += jnp.dot(att_r[src], wo[src, :, cols], preferred_element_type=F32)
            return carry

        lax.fori_loop(0, 4, tile, 0)

    for pos, src in enumerate(order):
        if pos:
            got(wo.at[src], wo_s.at[0], wo_r.at[src])

        def arrived(d, carry):
            at = (c + d) % 16
            got(att_r.at[src, pl.ds(at * 32, 32)], b_s.at[0, 0], b_r.at[src, at])
            return carry

        lax.fori_loop(0 if pos else 1, 16, arrived, 0)
        out_part(src)

    norm_rows(n2, gains[0, 1:2, :], ())
    ag_start(n2, m_s, m_r)
    loads[2].wait()
    loads[3].wait()

    def down(pos, row0, rows, target):
        return jnp.dot(
            act[pos, pl.ds(row0, rows), :],
            wd[:, pl.ds(pl.multiple_of(target * 256, 256), 256)],
            preferred_element_type=F32,
        )

    def mine(pos, row0, rows, target):
        value = down(pos, row0, rows, target)
        if pos == 0:
            value = value + x0[pl.ds(row0, rows), pl.ds(pl.multiple_of(target * 256, 256), 256)]
        return value

    def mlp(pos):
        r = order[pos]

        def tile(n, carry):
            cols = pl.ds(pl.multiple_of(n * 256, 256), 256)
            g = jnp.dot(n2[r], wgu[0, :, cols], preferred_element_type=F32)
            u = jnp.dot(n2[r], wgu[1, :, cols], preferred_element_type=F32)
            act[pos, :, cols] = (g / (1.0 + jnp.exp(-g)) * u).astype(BF16)
            return carry

        lax.fori_loop(0, 4, tile, 0)
        ds2[pos] = mine(pos, 0, 512, ho).astype(BF16)
        send(ds2.at[pos, top], dfl.at[r], d_s.at[pos, 0], d_r.at[r, 0], right)
        send(ds2.at[pos, bot], dfr.at[r], d_s.at[pos, 1], d_r.at[r, 1], left)
        dsr[pos, bot, :] = mine(pos, 256, 256, hr).astype(BF16)
        send(dsr.at[pos, bot], drl.at[r, bot], d_s.at[pos, 2], d_r.at[r, 2], right)
        dsl[pos, top, :] = mine(pos, 0, 256, hl).astype(BF16)
        send(dsl.at[pos, top], drr.at[r, top], d_s.at[pos, 3], d_r.at[r, 3], left)
        oacc[pos] = mine(pos, 0, 512, h)

    def pass_right(pos):
        r = order[pos]
        got(dfl.at[r], d_s.at[pos, 0], d_r.at[r, 0])
        dsr[pos, top, :] = (mine(pos, 0, 256, hr) + dfl[r].astype(F32)).astype(BF16)
        send(dsr.at[pos, top], drl.at[r, top], d_s.at[pos, 4], d_r.at[r, 4], right)

    def pass_left(pos):
        r = order[pos]
        got(dfr.at[r], d_s.at[pos, 1], d_r.at[r, 1])
        dsl[pos, bot, :] = (mine(pos, 256, 256, hl) + dfr[r].astype(F32)).astype(BF16)
        send(dsl.at[pos, bot], drr.at[r, bot], d_s.at[pos, 5], d_r.at[r, 5], left)

    mlp(0)
    ag_forward(n2, m_s, m_r)
    ag_wait(n2, m_s, m_r, 1)
    mlp(1)
    ag_wait(n2, m_s, m_r, 2)
    mlp(2)
    pass_right(1)
    pass_left(2)
    ag_wait(n2, m_s, m_r, 3)
    mlp(3)
    pass_right(3)
    pass_left(0)
    pass_right(0)
    pass_left(3)
    pass_right(2)
    pass_left(1)

    writes = []
    for pos in (1, 2, 0, 3):
        r = order[pos]
        for i, ref in ((2, drl.at[r, bot]), (3, drr.at[r, top]), (4, drl.at[r, top]), (5, drr.at[r, bot])):
            got(ref, d_s.at[pos, i], d_r.at[r, i])
        oacc[pos] = oacc[pos] + drl[r].astype(F32) + drr[r].astype(F32)
        w = pltpu.make_async_copy(oacc.at[pos], out.at[r], o_s.at[pos])
        w.start()
        writes.append(w)

    for s in sends:
        s.wait_send()

    def sent(d, carry):
        for r in range(4):
            at = (c + d) % 16
            rc(qs.at[r, pl.ds(at * 32, 32)], qr.at[r, c], a_s.at[r, at], a_r.at[r, c], right).wait_send()
        return carry

    lax.fori_loop(1, 16, sent, 0)

    def returned(d, carry):
        for j in range(1, 4):
            r = (h + j) % 4
            rc(att_s.at[r, d], att_r.at[h, pl.ds(c * 32, 32)], b_s.at[r, d], b_r.at[h, c], right).wait_send()
        return carry

    lax.fori_loop(0, 16, returned, 0)

    def returned_own(d, carry):
        at = (c + d) % 16
        rc(att_s.at[h, at], att_r.at[h, pl.ds(c * 32, 32)], b_s.at[h, at], b_r.at[h, c], right).wait_send()
        return carry

    lax.fori_loop(1, 16, returned_own, 0)
    for w in writes:
        w.wait()


def body(temporal, frame_ids, proj_weight, embed_table, qkv_weight, out_weight, gate_up, down_weight, norm_gains):
    c = lax.axis_index("codebook")
    h = lax.axis_index("hidden")
    start_id = embed_table.shape[1] - 1
    own_ids = lax.dynamic_slice_in_dim(frame_ids[:, 0], h * 512, 512, 0)
    earlier = lax.ppermute(own_ids, "codebook", [(i, i + 1) for i in range(15)])
    previous = jnp.where(c == 0, start_id, earlier)
    emb = embed_table[0][previous]
    vm, dma = pltpu.VMEM, pltpu.SemaphoreType.DMA
    any_spec = pl.BlockSpec(memory_space=pl.ANY)
    result = pl.pallas_call(
        kernel,
        name="depth_layer",
        out_shape=jax.ShapeDtypeStruct((4, 512, 256), F32),
        in_specs=[any_spec] * 7 + [pl.BlockSpec(memory_space=pltpu.VMEM)],
        out_specs=any_spec,
        scratch_shapes=[
            vm((2048, 1024), BF16), vm((1024, 1024), BF16), vm((3, 1024, 256), BF16), vm((4, 256, 1024), BF16),
            vm((2, 1024, 1024), BF16), vm((1024, 1024), BF16), vm((512, 1024), BF16),
            vm((512, 1024), BF16), vm((512, 1024), BF16), vm((512, 1024), BF16),
            vm((256, 1024), BF16), vm((256, 1024), BF16), vm((512, 1024), BF16), vm((512, 1024), BF16),
            vm((512, 1024), F32),
            vm((4, 512, 1024), BF16), vm((4, 512, 768), BF16), vm((4, 16, 32, 768), BF16),
            vm((4, 16, 32, 256), BF16), vm((4, 512, 256), BF16), vm((256, 256), F32),
            vm((4, 512, 1024), BF16), vm((4, 512, 1024), BF16),
            vm((4, 512, 256), BF16), vm((4, 512, 256), BF16), vm((4, 512, 256), BF16),
            vm((4, 256, 256), BF16), vm((4, 256, 256), BF16), vm((4, 512, 256), BF16), vm((4, 512, 256), BF16),
            vm((4, 512, 256), F32),
            dma((7,)), dma((15,)), dma((16,)), dma((3,)), dma((4,)), dma((6,)), dma((6,)),
            dma((6,)), dma((6,)), dma((6,)), dma((6,)), dma((4, 16)), dma((4, 16)), dma((4, 16)), dma((4, 16)),
            dma((4, 6)), dma((4, 6)), dma((4,)),
        ],
        compiler_params=pltpu.CompilerParams(
            collective_id=0, has_side_effects=True, vmem_limit_bytes=67043328
        ),
    )(temporal, emb, proj_weight, qkv_weight, out_weight, gate_up, down_weight, norm_gains)
    return result.reshape(1, 2048, 256)


def solution(mesh):
    placed = (
        P(("frames", "codebook"), "hidden"),
        P("frames", "codebook"),
        P("codebook", "hidden", None),
        P("codebook", None, None),
        P("codebook", None, None, "hidden"),
        P("codebook", "hidden", None),
        P("codebook", None, None, "hidden"),
        P("codebook", "hidden", None),
        P("codebook", None, None),
    )
    return jax.shard_map(
        body,
        mesh=mesh,
        in_specs=placed,
        out_specs=P("codebook", "frames", "hidden"),
        check_vma=False,
    )
```

```python
import functools

import jax
import jax.numpy as jnp
from jax import lax
from jax.experimental import pallas as pl
from jax.experimental.pallas import tpu as pltpu
from jax.sharding import PartitionSpec as P

HEADS = 16
MESH = pl.DeviceIdType.MESH
F32 = jnp.float32
BF16 = jnp.bfloat16
CHIPS = ((0, 1), (0, 3), (1, 0), (0, 2), (1, 1), (1, 3), (1, 2))


def kernel(
    temporal, emb_in, wp_in, wqkv_in, wo_in, wgu_in, wd_in, gains, out,
    tbuf, wp, wqkv, wo, wgu, wd, emb,
    ps2, psr, psl, pfl, pfr, prl, prr, x0,
    n1, qs, qr, att_s, att_r, bias,
    n2, act, ds2, dsr, dsl, dfl, dfr, drl, drr, oacc,
    loc, t_s, t_r, wo_s, wo_r, p_s, p_r, n_s, n_r, m_s, m_r, a_s, a_r, b_s, b_r, d_s, d_r, o_s,
):
    f = lax.axis_index("frames")
    c = lax.axis_index("codebook")
    h = lax.axis_index("hidden")
    hr, hl, ho = (h + 1) % 4, (h + 3) % 4, (h + 2) % 4
    right, left = (f, c, hr), (f, c, hl)
    y, x, k = c // 8, (c // 2) % 4, c % 2
    order = (h, hl, hr, ho)
    top, bot = pl.ds(0, 128), pl.ds(128, 128)
    sends = []

    def rc(src, dst, ss, rs, dev):
        return pltpu.make_async_remote_copy(
            src_ref=src, dst_ref=dst, send_sem=ss, recv_sem=rs, device_id=dev, device_id_type=MESH
        )

    def send(src, dst, ss, rs, dev):
        s = rc(src, dst, ss, rs, dev)
        s.start()
        sends.append(s)

    def got(ref, ss, rs):
        rc(ref, ref, ss, rs, right).wait_recv()

    loads = [
        pltpu.make_async_copy(s, d, loc.at[i])
        for i, (s, d) in enumerate((
            (wp_in.at[0], wp), (wqkv_in.at[0], wqkv), (wgu_in.at[0], wgu), (wd_in.at[0], wd), (emb_in, emb),
            (wo_in.at[0], wo.at[h]), (temporal.at[0], tbuf.at[0, c]), (temporal.at[1], tbuf.at[1, c]),
        ))
    ]
    for i in (6, 7, 0, 4, 5, 1, 2, 3):
        loads[i].start()

    barrier = pltpu.get_barrier_semaphore()

    def greet(n, carry):
        pl.semaphore_signal(
            barrier, inc=1, device_id=(f, (c + n // 4) % 16, (h + n % 4) % 4), device_id_type=MESH
        )
        return carry

    lax.fori_loop(1, 64, greet, 0)
    pl.semaphore_wait(barrier, 63)

    partner = (f, y * 8 + x * 2 + 1 - k, h)

    def temporal_out(q):
        loads[6 + q].wait()
        for i, (dy, dx) in enumerate(CHIPS):
            dst = ((y + dy) % 2) * 8 + ((x + dx) % 4) * 2 + k
            send(tbuf.at[q, c], tbuf.at[q, c], t_s.at[q, i], t_r.at[q, c], (f, dst, h))
        send(tbuf.at[q, c], tbuf.at[q, c], t_s.at[q, 7], t_r.at[q, c], partner)

    def temporal_in(q):
        for i, (dy, dx) in enumerate(CHIPS):
            src = ((y + 2 - dy) % 2) * 8 + ((x + 4 - dx) % 4) * 2 + k
            got(tbuf.at[q, src], t_s.at[q, 0], t_r.at[q, src])
            send(tbuf.at[q, src], tbuf.at[q, src], t_s.at[q, 8 + i], t_r.at[q, src], partner)
        for dy, dx in ((0, 0),) + CHIPS:
            src = ((y + dy) % 2) * 8 + ((x + dx) % 4) * 2 + 1 - k
            got(tbuf.at[q, src], t_s.at[q, 0], t_r.at[q, src])

    def proj(q, block, row0, rows, store):
        def tile(n, carry):
            cols = pl.ds(pl.multiple_of(n * 256, 256), 256)
            lhs = tbuf[q, pl.ds(block * 4 + row0 // 64, rows // 64)].reshape(rows, 1024)
            store(cols, jnp.dot(lhs, wp[:, cols], preferred_element_type=F32))
            return carry

        lax.fori_loop(0, 4, tile, 0)

    def into(ref, row0, rows, extra=None):
        def store(cols, value):
            if extra is not None:
                value = value + extra[:, cols].astype(F32)
            ref[pl.ds(row0, rows), cols] = value.astype(ref.dtype)

        return store

    def proj_far(q):
        ss, rs = p_s.at[q], p_r.at[q]
        proj(q, ho, 0, 256, into(ps2.at[q], 0, 256))
        send(ps2.at[q, top], pfl.at[q], ss.at[0], rs.at[0], right)
        send(ps2.at[q, bot], pfr.at[q], ss.at[1], rs.at[1], left)

    def proj_near(q):
        ss, rs = p_s.at[q], p_r.at[q]
        proj(q, hr, 128, 128, into(psr.at[q], 128, 128))
        send(psr.at[q, bot], prl.at[q, bot], ss.at[2], rs.at[2], right)
        proj(q, hl, 0, 128, into(psl.at[q], 0, 128))
        send(psl.at[q, top], prr.at[q, top], ss.at[3], rs.at[3], left)

    def proj_own(q):
        proj(q, h, 0, 256, into(x0.at[q], 0, 256, emb.at[q]))

    def proj_pass(q):
        ss, rs = p_s.at[q], p_r.at[q]
        got(pfl.at[q], ss.at[0], rs.at[0])
        proj(q, hr, 0, 128, into(psr.at[q], 0, 128, pfl.at[q]))
        send(psr.at[q, top], prl.at[q, top], ss.at[4], rs.at[4], right)
        got(pfr.at[q], ss.at[1], rs.at[1])
        proj(q, hl, 128, 128, into(psl.at[q], 128, 128, pfr.at[q]))
        send(psl.at[q, bot], prr.at[q, bot], ss.at[5], rs.at[5], left)

    def norm_rows(q, dst, gain, extras):
        def chunk(n, carry):
            rows = pl.ds(pl.multiple_of(n * 32, 32), 32)
            v = x0[q, rows, :]
            for e in extras:
                v = v + e[q, rows, :].astype(F32)
            if extras:
                x0[q, rows, :] = v
            scale = lax.rsqrt(jnp.mean(v * v, axis=-1, keepdims=True) + 1e-05)
            dst[q, h, rows, :] = (v * scale * gain).astype(BF16)
            return carry

        lax.fori_loop(0, 8, chunk, 0)

    def norm_one(q):
        for i, ref in ((2, prl.at[q, bot]), (3, prr.at[q, top]), (4, prl.at[q, top]), (5, prr.at[q, bot])):
            got(ref, p_s.at[q, i], p_r.at[q, i])
        norm_rows(q, n1, gains[0, 0:1, :], (prl, prr))

    def ag_start(buf, ss, rs):
        send(buf.at[h, top], buf.at[h, top], ss.at[0], rs.at[0], right)
        send(buf.at[h, bot], buf.at[h, bot], ss.at[2], rs.at[2], left)
        send(buf.at[h, bot], buf.at[h, bot], ss.at[1], rs.at[1], right)
        send(buf.at[h, top], buf.at[h, top], ss.at[3], rs.at[3], left)

    def ag_forward(buf, ss, rs):
        got(buf.at[hl, top], ss.at[0], rs.at[0])
        send(buf.at[hl, top], buf.at[hl, top], ss.at[4], rs.at[4], right)
        got(buf.at[hr, bot], ss.at[2], rs.at[2])
        send(buf.at[hr, bot], buf.at[hr, bot], ss.at[5], rs.at[5], left)

    def ag_wait(buf, ss, rs, pos):
        if pos == 1:
            got(buf.at[hl, bot], ss.at[1], rs.at[1])
        if pos == 2:
            got(buf.at[hr, top], ss.at[3], rs.at[3])
        if pos == 3:
            got(buf.at[ho, top], ss.at[4], rs.at[4])
            got(buf.at[ho, bot], ss.at[5], rs.at[5])

    ag_one = lambda q: (n1.at[q], n_s.at[q], n_r.at[q])
    ag_two = lambda q: (n2.at[q], m_s.at[q], m_r.at[q])

    def peer(d):
        return ((y + d // 8) % 2) * 8 + ((x + (d // 2) % 4) % 4) * 2 + (k + d) % 2

    def qkv(q, pos):
        r = order[pos]
        ag_wait(*ag_one(q), pos)
        for i in range(3):
            part = jnp.dot(n1[q, r], wqkv[i], preferred_element_type=F32)
            qs[q, r, :, i * 256:(i + 1) * 256] = part.astype(BF16)

        def post(d, carry):
            dst = peer(d)
            rc(
                qs.at[q, r, pl.ds(dst * 16, 16)], qr.at[q, r, c], a_s.at[q, r], a_r.at[q, r], (f, dst, h)
            ).start()
            return carry

        lax.fori_loop(1, 16, post, 0)
        qr[q, r, c] = qs[q, r, pl.ds(pl.multiple_of(c * 16, 16), 16), :]

    def attend(q, pos):
        r = order[pos]
        got(qr.at[q, r, pl.ds(0, 15)], a_s.at[q, r], a_r.at[q, r])

        def unit(n, carry):
            pair = n * 128
            take = lambda i: qr[
                q, r, :, :, pl.ds(pl.multiple_of(i * 256 + pair, 128), 128)
            ].reshape(256, 128)
            qq, kk, v = take(0), take(1), take(2)
            lane = lax.broadcasted_iota(jnp.int32, (256, 128), 1)
            halves = []
            for half in range(2):
                mine = (lane // 64) == half
                qh = jnp.where(mine, qq, jnp.zeros_like(qq))
                parts = []
                for rows, width in ((slice(0, 128), 128), (slice(128, 256), 256)):
                    s = lax.dot_general(
                        qh[rows], kk[:width], (((1,), (1,)), ((), ())), preferred_element_type=F32
                    )
                    s = s * 0.125 + bias[rows, :width]
                    e = jnp.exp(s - jnp.max(s, axis=-1, keepdims=True))
                    total = jnp.sum(e, axis=-1, keepdims=True)
                    o = jnp.dot(e.astype(BF16), v[:width], preferred_element_type=F32)
                    parts.append(o / total)
                halves.append(jnp.concatenate(parts, axis=0))
            o = jnp.where((lane // 64) == 0, halves[0], halves[1]).astype(BF16)
            att_s[q, r, :, :, pl.ds(pl.multiple_of(pair, 128), 128)] = o.reshape(16, 16, 128)
            return carry

        lax.fori_loop(0, 2, unit, 0)

        def post(d, carry):
            dst = peer(d)
            rc(
                att_s.at[q, r, dst], att_r.at[q, h, pl.ds(c * 16, 16)], b_s.at[q, r], b_r.at[q, h], (f, dst, r)
            ).start()
            return carry

        lax.fori_loop(0 if pos else 1, 16, post, 0)
        if pos == 0:
            att_r[q, h, pl.ds(pl.multiple_of(c * 16, 16), 16), :] = att_s[q, h, c]

    def out_proj(q):
        for pos, src in enumerate(order):
            got(att_r.at[q, src, pl.ds(0, 256 if pos else 240)], b_s.at[q, src], b_r.at[q, src])

        def tile(n, carry):
            cols = pl.ds(pl.multiple_of(n * 256, 256), 256)
            total = x0[q, :, cols]
            for src in range(4):
                total = total + jnp.dot(att_r[q, src], wo[src, :, cols], preferred_element_type=F32)
            x0[q, :, cols] = total
            return carry

        lax.fori_loop(0, 4, tile, 0)
        norm_rows(q, n2, gains[0, 1:2, :], ())
        ag_start(*ag_two(q))

    def mine(q, pos, row0, rows, target):
        cols = pl.ds(pl.multiple_of(target * 256, 256), 256)
        value = jnp.dot(act[q, pos, pl.ds(row0, rows), :], wd[:, cols], preferred_element_type=F32)
        if pos == 0:
            value = value + x0[q, pl.ds(row0, rows), cols]
        return value

    def mlp(q, pos):
        r = order[pos]
        ss, rs = d_s.at[q, pos], d_r.at[q, r]
        ag_wait(*ag_two(q), pos)

        def tile(n, carry):
            cols = pl.ds(pl.multiple_of(n * 256, 256), 256)
            g = jnp.dot(n2[q, r], wgu[0, :, cols], preferred_element_type=F32)
            u = jnp.dot(n2[q, r], wgu[1, :, cols], preferred_element_type=F32)
            act[q, pos, :, cols] = (g / (1.0 + jnp.exp(-g)) * u).astype(BF16)
            return carry

        lax.fori_loop(0, 4, tile, 0)
        ds2[q, pos] = mine(q, pos, 0, 256, ho).astype(BF16)
        send(ds2.at[q, pos, top], dfl.at[q, r], ss.at[0], rs.at[0], right)
        send(ds2.at[q, pos, bot], dfr.at[q, r], ss.at[1], rs.at[1], left)
        dsr[q, pos, bot, :] = mine(q, pos, 128, 128, hr).astype(BF16)
        send(dsr.at[q, pos, bot], drl.at[q, r, bot], ss.at[2], rs.at[2], right)
        dsl[q, pos, top, :] = mine(q, pos, 0, 128, hl).astype(BF16)
        send(dsl.at[q, pos, top], drr.at[q, r, top], ss.at[3], rs.at[3], left)
        oacc[q, pos] = mine(q, pos, 0, 256, h).reshape(4, 64, 256)

    def pass_right(q, pos):
        r = order[pos]
        ss, rs = d_s.at[q, pos], d_r.at[q, r]
        got(dfl.at[q, r], ss.at[0], rs.at[0])
        dsr[q, pos, top, :] = (mine(q, pos, 0, 128, hr) + dfl[q, r].astype(F32)).astype(BF16)
        send(dsr.at[q, pos, top], drl.at[q, r, top], ss.at[4], rs.at[4], right)

    def pass_left(q, pos):
        r = order[pos]
        ss, rs = d_s.at[q, pos], d_r.at[q, r]
        got(dfr.at[q, r], ss.at[1], rs.at[1])
        dsl[q, pos, bot, :] = (mine(q, pos, 128, 128, hl) + dfr[q, r].astype(F32)).astype(BF16)
        send(dsl.at[q, pos, bot], drr.at[q, r, bot], ss.at[5], rs.at[5], left)

    writes = []

    def finish(q, pos):
        r = order[pos]
        for i, ref in (
            (2, drl.at[q, r, bot]), (3, drr.at[q, r, top]), (4, drl.at[q, r, top]), (5, drr.at[q, r, bot])
        ):
            got(ref, d_s.at[q, pos, i], d_r.at[q, r, i])
        gathered = drl[q, r].astype(F32) + drr[q, r].astype(F32)
        oacc[q, pos] = oacc[q, pos] + gathered.reshape(4, 64, 256)
        w = pltpu.make_async_copy(oacc.at[q, pos], out.at[r, :, q], o_s.at[q, pos])
        w.start()
        writes.append(w)

    temporal_out(0)
    temporal_out(1)
    loads[5].wait()
    for j in (1, 3, 2):
        send(wo.at[h], wo.at[h], wo_s.at[j - 1], wo_r.at[h], (f, c, (h + j) % 4))
    row = lax.broadcasted_iota(jnp.int32, (256, 256), 0)
    col = lax.broadcasted_iota(jnp.int32, (256, 256), 1)
    bias[...] = jnp.where((row % 16 == col % 16) & (row // 16 >= col // 16), 0.0, -1e30)
    loads[0].wait()
    temporal_in(0)
    proj_far(0)
    proj_near(0)
    loads[4].wait()
    proj_own(0)
    proj_pass(0)
    temporal_in(1)
    proj_far(1)
    norm_one(0)
    ag_start(*ag_one(0))
    loads[1].wait()
    qkv(0, 0)
    proj_near(1)
    proj_own(1)
    ag_forward(*ag_one(0))
    proj_pass(1)
    attend(0, 0)
    qkv(0, 1)
    qkv(0, 2)
    qkv(0, 3)
    attend(0, 1)
    attend(0, 2)
    norm_one(1)
    ag_start(*ag_one(1))
    qkv(1, 0)
    attend(0, 3)
    for src in order[1:]:
        got(wo.at[src], wo_s.at[0], wo_r.at[src])
    out_proj(0)
    ag_forward(*ag_one(1))
    loads[2].wait()
    loads[3].wait()
    mlp(0, 0)
    attend(1, 0)
    qkv(1, 1)
    qkv(1, 2)
    ag_forward(*ag_two(0))
    qkv(1, 3)
    attend(1, 1)
    attend(1, 2)
    mlp(0, 1)
    mlp(0, 2)
    attend(1, 3)
    pass_right(0, 1)
    pass_left(0, 2)
    out_proj(1)
    mlp(1, 0)
    mlp(0, 3)
    pass_right(0, 3)
    pass_left(0, 0)
    pass_right(0, 0)
    pass_left(0, 3)
    pass_right(0, 2)
    pass_left(0, 1)
    ag_forward(*ag_two(1))
    mlp(1, 1)
    mlp(1, 2)
    pass_right(1, 1)
    pass_left(1, 2)
    for pos in (1, 2, 0, 3):
        finish(0, pos)
    mlp(1, 3)
    pass_right(1, 3)
    pass_left(1, 0)
    pass_right(1, 0)
    pass_left(1, 3)
    pass_right(1, 2)
    pass_left(1, 1)
    for pos in (1, 2, 0, 3):
        finish(1, pos)

    for s in sends:
        s.wait_send()
    for q in range(2):
        for pos, r in enumerate(order):
            block = qs.at[q, r, pl.ds(0, 240)]
            rc(block, block, a_s.at[q, r], a_r.at[q, r], right).wait_send()
            block = att_s.at[q, r, pl.ds(0, 16 if pos else 15)]
            rc(block, block, b_s.at[q, r], b_r.at[q, r], right).wait_send()
    for w in writes:
        w.wait()


def body(temporal, frame_ids, proj_weight, embed_table, qkv_weight, out_weight, gate_up, down_weight, norm_gains):
    c = lax.axis_index("codebook")
    h = lax.axis_index("hidden")
    start_id = embed_table.shape[1] - 1
    own_ids = lax.dynamic_slice_in_dim(frame_ids[:, 0], h * 512, 512, 0)
    own_ids = own_ids.reshape(4, 2, 64).transpose(1, 0, 2).reshape(512)
    earlier = lax.ppermute(own_ids, "codebook", [(i, i + 1) for i in range(15)])
    previous = jnp.where(c == 0, start_id, earlier)
    emb = embed_table[0][previous].reshape(2, 256, 1024)
    vm, dma = pltpu.VMEM, pltpu.SemaphoreType.DMA
    any_spec = pl.BlockSpec(memory_space=pl.ANY)
    result = pl.pallas_call(
        kernel,
        name="depth_layer",
        out_shape=jax.ShapeDtypeStruct((4, 4, 2, 64, 256), F32),
        in_specs=[any_spec] * 7 + [pl.BlockSpec(memory_space=pltpu.VMEM)],
        out_specs=any_spec,
        scratch_shapes=[
            vm((2, 16, 64, 1024), BF16), vm((1024, 1024), BF16), vm((3, 1024, 256), BF16), vm((4, 256, 1024), BF16),
            vm((2, 1024, 1024), BF16), vm((1024, 1024), BF16), vm((2, 256, 1024), BF16),
            vm((2, 256, 1024), BF16), vm((2, 256, 1024), BF16), vm((2, 256, 1024), BF16),
            vm((2, 128, 1024), BF16), vm((2, 128, 1024), BF16), vm((2, 256, 1024), BF16), vm((2, 256, 1024), BF16),
            vm((2, 256, 1024), F32),
            vm((2, 4, 256, 1024), BF16), vm((2, 4, 256, 768), BF16), vm((2, 4, 16, 16, 768), BF16),
            vm((2, 4, 16, 16, 256), BF16), vm((2, 4, 256, 256), BF16), vm((256, 256), F32),
            vm((2, 4, 256, 1024), BF16), vm((2, 4, 256, 1024), BF16),
            vm((2, 4, 256, 256), BF16), vm((2, 4, 256, 256), BF16), vm((2, 4, 256, 256), BF16),
            vm((2, 4, 128, 256), BF16), vm((2, 4, 128, 256), BF16),
            vm((2, 4, 256, 256), BF16), vm((2, 4, 256, 256), BF16),
            vm((2, 4, 4, 64, 256), F32),
            dma((8,)), dma((2, 15)), dma((2, 16)), dma((3,)), dma((4,)), dma((2, 6)), dma((2, 6)),
            dma((2, 6)), dma((2, 6)), dma((2, 6)), dma((2, 6)), dma((2, 4)), dma((2, 4)), dma((2, 4)), dma((2, 4)),
            dma((2, 4, 6)), dma((2, 4, 6)), dma((2, 4)),
        ],
        compiler_params=pltpu.CompilerParams(
            collective_id=0, has_side_effects=True, vmem_limit_bytes=67043328
        ),
    )(
        temporal.reshape(2, 64, 1024), emb, proj_weight, qkv_weight, out_weight, gate_up, down_weight, norm_gains
    )
    return result.reshape(1, 2048, 256)


def solution(mesh):
    placed = (
        P(("frames", "codebook"), "hidden"),
        P("frames", "codebook"),
        P("codebook", "hidden", None),
        P("codebook", None, None),
        P("codebook", None, None, "hidden"),
        P("codebook", "hidden", None),
        P("codebook", None, None, "hidden"),
        P("codebook", "hidden", None),
        P("codebook", None, None),
    )
    return jax.shard_map(
        body,
        mesh=mesh,
        in_specs=placed,
        out_specs=P("codebook", "frames", "hidden"),
        check_vma=False,
    )
```

```python
import functools

import jax
import jax.numpy as jnp
from jax import lax
from jax.experimental import pallas as pl
from jax.experimental.pallas import tpu as pltpu
from jax.sharding import PartitionSpec as P

HEADS = 16
MESH = pl.DeviceIdType.MESH
F32 = jnp.float32
BF16 = jnp.bfloat16
CHIPS = ((0, 1), (0, 3), (1, 0), (0, 2), (1, 1), (1, 3), (1, 2))


def kernel(
    temporal, emb_in, wp_in, wqkv_in, wo_in, wgu_in, wd_in, gains, out,
    tbuf, wp, wq, wo, wgu, wd, emb,
    ps2, psr, psl, pfl, pfr, prl, prr, x0,
    n1, nq, qs, qr, att_s, att_r, bias,
    n2, act, ds2, dsr, dsl, dfl, dfr, drl, drr, oacc,
    loc, t_s, t_r, wo_s, wo_r, p_s, p_r, w_s, w_r, v_s, v_r, x_s, x_r, m_s, m_r, a_s, a_r, b_s, b_r, d_s, d_r, o_s,
):
    f = lax.axis_index("frames")
    c = lax.axis_index("codebook")
    h = lax.axis_index("hidden")
    hr, hl, ho = (h + 1) % 4, (h + 3) % 4, (h + 2) % 4
    right, left = (f, c, hr), (f, c, hl)
    y, x, k = c // 8, (c // 2) % 4, c % 2
    order = (h, hl, hr, ho)
    top, bot = pl.ds(0, 128), pl.ds(128, 128)
    sends = []

    def rc(src, dst, ss, rs, dev):
        return pltpu.make_async_remote_copy(
            src_ref=src, dst_ref=dst, send_sem=ss, recv_sem=rs, device_id=dev, device_id_type=MESH
        )

    def send(src, dst, ss, rs, dev):
        s = rc(src, dst, ss, rs, dev)
        s.start()
        sends.append(s)

    def got(ref, ss, rs):
        rc(ref, ref, ss, rs, right).wait_recv()

    loads = [
        pltpu.make_async_copy(s, d, loc.at[i])
        for i, (s, d) in enumerate((
            (wp_in.at[0], wp), (wqkv_in.at[0], wq.at[h]), (wgu_in.at[0], wgu), (wd_in.at[0], wd), (emb_in, emb),
            (wo_in.at[0], wo.at[h]), (temporal.at[0], tbuf.at[0, c]), (temporal.at[1], tbuf.at[1, c]),
        ))
    ]
    home = k == f
    worker = f * 8 + y * 4 + x
    book = c - k + f
    for i in (6, 7, 0, 4, 5, 2, 3):
        loads[i].start()

    @pl.when(home)
    def _():
        loads[1].start()

    barrier = pltpu.get_barrier_semaphore()

    def greet(n, carry):
        pl.semaphore_signal(
            barrier, inc=1, device_id=((f + n // 16) % 2, (c + n % 16) % 16, h), device_id_type=MESH
        )
        return carry

    pl.semaphore_signal(barrier, inc=1, device_id=right, device_id_type=MESH)
    pl.semaphore_signal(barrier, inc=1, device_id=left, device_id_type=MESH)
    lax.fori_loop(1, 32, greet, 0)
    pl.semaphore_wait(barrier, 33)

    partner = (f, y * 8 + x * 2 + 1 - k, h)

    def temporal_out(q):
        loads[6 + q].wait()
        for i, (dy, dx) in enumerate(CHIPS):
            dst = ((y + dy) % 2) * 8 + ((x + dx) % 4) * 2 + k
            send(tbuf.at[q, c], tbuf.at[q, c], t_s.at[q, i], t_r.at[q, c], (f, dst, h))
        send(tbuf.at[q, c], tbuf.at[q, c], t_s.at[q, 7], t_r.at[q, c], partner)

    def temporal_in(q):
        for i, (dy, dx) in enumerate(CHIPS):
            src = ((y + 2 - dy) % 2) * 8 + ((x + 4 - dx) % 4) * 2 + k
            got(tbuf.at[q, src], t_s.at[q, 0], t_r.at[q, src])
            send(tbuf.at[q, src], tbuf.at[q, src], t_s.at[q, 8 + i], t_r.at[q, src], partner)
        for dy, dx in ((0, 0),) + CHIPS:
            src = ((y + dy) % 2) * 8 + ((x + dx) % 4) * 2 + 1 - k
            got(tbuf.at[q, src], t_s.at[q, 0], t_r.at[q, src])

    def proj(q, block, row0, rows, store):
        def tile(n, carry):
            cols = pl.ds(pl.multiple_of(n * 256, 256), 256)
            lhs = tbuf[q, pl.ds(block * 4 + row0 // 64, rows // 64)].reshape(rows, 1024)
            store(cols, jnp.dot(lhs, wp[:, cols], preferred_element_type=F32))
            return carry

        lax.fori_loop(0, 4, tile, 0)

    def into(ref, row0, rows, extra=None):
        def store(cols, value):
            if extra is not None:
                value = value + extra[:, cols].astype(F32)
            ref[pl.ds(row0, rows), cols] = value.astype(ref.dtype)

        return store

    def proj_far(q):
        ss, rs = p_s.at[q], p_r.at[q]
        proj(q, ho, 0, 256, into(ps2.at[q], 0, 256))
        send(ps2.at[q, top], pfl.at[q], ss.at[0], rs.at[0], right)
        send(ps2.at[q, bot], pfr.at[q], ss.at[1], rs.at[1], left)

    def proj_near(q):
        ss, rs = p_s.at[q], p_r.at[q]
        proj(q, hr, 128, 128, into(psr.at[q], 128, 128))
        send(psr.at[q, bot], prl.at[q, bot], ss.at[2], rs.at[2], right)
        proj(q, hl, 0, 128, into(psl.at[q], 0, 128))
        send(psl.at[q, top], prr.at[q, top], ss.at[3], rs.at[3], left)

    def proj_own(q):
        proj(q, h, 0, 256, into(x0.at[q], 0, 256, emb.at[q]))

    def proj_pass(q):
        ss, rs = p_s.at[q], p_r.at[q]
        got(pfl.at[q], ss.at[0], rs.at[0])
        proj(q, hr, 0, 128, into(psr.at[q], 0, 128, pfl.at[q]))
        send(psr.at[q, top], prl.at[q, top], ss.at[4], rs.at[4], right)
        got(pfr.at[q], ss.at[1], rs.at[1])
        proj(q, hl, 128, 128, into(psl.at[q], 128, 128, pfr.at[q]))
        send(psl.at[q, bot], prr.at[q, bot], ss.at[5], rs.at[5], left)

    def norm_rows(q, dst, gain, extras):
        def chunk(n, carry):
            rows = pl.ds(pl.multiple_of(n * 32, 32), 32)
            v = x0[q, rows, :]
            for e in extras:
                v = v + e[q, rows, :].astype(F32)
            if extras:
                x0[q, rows, :] = v
            scale = lax.rsqrt(jnp.mean(v * v, axis=-1, keepdims=True) + 1e-05)
            dst[rows, :] = (v * scale * gain).astype(BF16)
            return carry

        lax.fori_loop(0, 8, chunk, 0)

    def norm_one(q):
        for i, ref in ((2, prl.at[q, bot]), (3, prr.at[q, top]), (4, prl.at[q, top]), (5, prr.at[q, bot])):
            got(ref, p_s.at[q, i], p_r.at[q, i])

        @pl.when(home)
        def _():
            norm_rows(q, nq.at[q], gains[0, 0:1, :], (prl, prr))

        @pl.when(jnp.logical_not(home))
        def _():
            norm_rows(q, n1.at[q], gains[0, 0:1, :], (prl, prr))
            swap(q).start()

    def swap(q):
        return rc(n1.at[q], nq.at[q], x_s.at[q], x_r.at[q], (1 - f, c - k + 1 - k, h))

    def swap_in(q):
        @pl.when(jnp.logical_not(home))
        def _():
            swap(q).wait_recv()

    def ag_start(buf, ss, rs):
        send(buf.at[h, top], buf.at[h, top], ss.at[0], rs.at[0], right)
        send(buf.at[h, bot], buf.at[h, bot], ss.at[2], rs.at[2], left)
        send(buf.at[h, bot], buf.at[h, bot], ss.at[1], rs.at[1], right)
        send(buf.at[h, top], buf.at[h, top], ss.at[3], rs.at[3], left)

    def ag_forward(buf, ss, rs):
        got(buf.at[hl, top], ss.at[0], rs.at[0])
        send(buf.at[hl, top], buf.at[hl, top], ss.at[4], rs.at[4], right)
        got(buf.at[hr, bot], ss.at[2], rs.at[2])
        send(buf.at[hr, bot], buf.at[hr, bot], ss.at[5], rs.at[5], left)

    def ag_wait(buf, ss, rs, pos):
        if pos == 1:
            got(buf.at[hl, bot], ss.at[1], rs.at[1])
        if pos == 2:
            got(buf.at[hr, top], ss.at[3], rs.at[3])
        if pos == 3:
            got(buf.at[ho, top], ss.at[4], rs.at[4])
            got(buf.at[ho, bot], ss.at[5], rs.at[5])

    ag_two = lambda q: (n2.at[q], m_s.at[q], m_r.at[q])

    upper, lower = pl.ds(0, 512), pl.ds(512, 512)

    def w_copy(i):
        part = lambda r, rows: wq.at[r, :, rows]
        block, dev = (
            (part(h, upper), right), (part(h, lower), right), (part(h, lower), left), (part(h, upper), left),
            (part(hl, upper), right), (part(hr, lower), left),
        )[i]
        return rc(block, block, w_s.at[i], w_r.at[i], dev)

    def w_share(pos):
        block = wq.at[order[pos]]
        return rc(block, block, v_s.at[pos], v_r.at[pos], partner)

    def w_start():
        @pl.when(home)
        def _():
            loads[1].wait()
            for i in (0, 2, 1, 3):
                w_copy(i).start()
            w_share(0).start()

    def w_forward():
        @pl.when(home)
        def _():
            got(wq.at[hl, :, upper], w_s.at[0], w_r.at[0])
            w_copy(4).start()
            got(wq.at[hr, :, lower], w_s.at[2], w_r.at[2])
            w_copy(5).start()

    def w_in(pos):
        @pl.when(home)
        def _():
            if pos == 1:
                got(wq.at[hl, :, lower], w_s.at[1], w_r.at[1])
            if pos == 2:
                got(wq.at[hr, :, upper], w_s.at[3], w_r.at[3])
            if pos == 3:
                got(wq.at[ho, :, upper], w_s.at[4], w_r.at[4])
                got(wq.at[ho, :, lower], w_s.at[5], w_r.at[5])
            if pos:
                w_share(pos).start()

        @pl.when(jnp.logical_not(home))
        def _():
            w_share(pos).wait_recv()

    def qkv(q, pos):
        r = order[pos]
        for i in range(3):
            part = jnp.dot(nq[q], wq[r, i], preferred_element_type=F32)
            qs[q, r, :, i * 256:(i + 1) * 256] = part.astype(BF16)

        def post(d, carry):
            df, dy, dx = (f + d // 8) % 2, (y + (d // 4) % 2) % 2, (x + d % 4) % 4
            rc(
                qs.at[q, r, pl.ds((df * 8 + dy * 4 + dx) * 16, 16)], qr.at[q, r, book],
                a_s.at[q, r], a_r.at[q, r], (df, dy * 8 + dx * 2 + k, h),
            ).start()
            return carry

        lax.fori_loop(1, 16, post, 0)
        qr[q, r, book] = qs[q, r, pl.ds(pl.multiple_of(worker * 16, 16), 16), :]

    def attend(q, pos):
        r = order[pos]
        got(qr.at[q, r, pl.ds(0, 15)], a_s.at[q, r], a_r.at[q, r])

        def unit(n, carry):
            pair = n * 128
            take = lambda i: qr[
                q, r, :, :, pl.ds(pl.multiple_of(i * 256 + pair, 128), 128)
            ].reshape(256, 128)
            qq, kk, v = take(0), take(1), take(2)
            lane = lax.broadcasted_iota(jnp.int32, (256, 128), 1)
            halves = []
            for half in range(2):
                mine = (lane // 64) == half
                qh = jnp.where(mine, qq, jnp.zeros_like(qq))
                parts = []
                for rows, width in ((slice(0, 128), 128), (slice(128, 256), 256)):
                    s = lax.dot_general(
                        qh[rows], kk[:width], (((1,), (1,)), ((), ())), preferred_element_type=F32
                    )
                    s = s * 0.125 + bias[rows, :width]
                    e = jnp.exp(s - jnp.max(s, axis=-1, keepdims=True))
                    total = jnp.sum(e, axis=-1, keepdims=True)
                    o = jnp.dot(e.astype(BF16), v[:width], preferred_element_type=F32)
                    parts.append(o / total)
                halves.append(jnp.concatenate(parts, axis=0))
            o = jnp.where((lane // 64) == 0, halves[0], halves[1]).astype(BF16)
            att_s[q, r, :, :, pl.ds(pl.multiple_of(pair, 128), 128)] = o.reshape(16, 16, 128)
            return carry

        lax.fori_loop(0, 2, unit, 0)

        def back(d):
            to = (c + d) % 16
            return rc(
                att_s.at[q, r, to], att_r.at[q, r, pl.ds(worker * 16, 16)], b_s.at[q, r], b_r.at[q, r], (k, to, h)
            )

        def post(d, carry):
            back(d).start()
            return carry

        lax.fori_loop(1, 16, post, 0)

        @pl.when(home)
        def _():
            att_r[q, r, pl.ds(pl.multiple_of(worker * 16, 16), 16), :] = att_s[q, r, c]

        @pl.when(jnp.logical_not(home))
        def _():
            back(0).start()

    def out_proj(q):
        for src in order:
            @pl.when(home)
            def _():
                got(att_r.at[q, src, pl.ds(0, 240)], b_s.at[q, src], b_r.at[q, src])

            @pl.when(jnp.logical_not(home))
            def _():
                got(att_r.at[q, src], b_s.at[q, src], b_r.at[q, src])

        def tile(n, carry):
            cols = pl.ds(pl.multiple_of(n * 256, 256), 256)
            total = x0[q, :, cols]
            for src in range(4):
                total = total + jnp.dot(att_r[q, src], wo[src, :, cols], preferred_element_type=F32)
            x0[q, :, cols] = total
            return carry

        lax.fori_loop(0, 4, tile, 0)
        norm_rows(q, n2.at[q, h], gains[0, 1:2, :], ())
        ag_start(*ag_two(q))

    def mine(q, pos, row0, rows, target):
        cols = pl.ds(pl.multiple_of(target * 256, 256), 256)
        value = jnp.dot(act[q, pos, pl.ds(row0, rows), :], wd[:, cols], preferred_element_type=F32)
        if pos == 0:
            value = value + x0[q, pl.ds(row0, rows), cols]
        return value

    def mlp(q, pos):
        r = order[pos]
        ss, rs = d_s.at[q, pos], d_r.at[q, r]
        ag_wait(*ag_two(q), pos)

        def tile(n, carry):
            cols = pl.ds(pl.multiple_of(n * 256, 256), 256)
            g = jnp.dot(n2[q, r], wgu[0, :, cols], preferred_element_type=F32)
            u = jnp.dot(n2[q, r], wgu[1, :, cols], preferred_element_type=F32)
            act[q, pos, :, cols] = (g / (1.0 + jnp.exp(-g)) * u).astype(BF16)
            return carry

        lax.fori_loop(0, 4, tile, 0)
        ds2[q, pos] = mine(q, pos, 0, 256, ho).astype(BF16)
        send(ds2.at[q, pos, top], dfl.at[q, r], ss.at[0], rs.at[0], right)
        send(ds2.at[q, pos, bot], dfr.at[q, r], ss.at[1], rs.at[1], left)
        dsr[q, pos, bot, :] = mine(q, pos, 128, 128, hr).astype(BF16)
        send(dsr.at[q, pos, bot], drl.at[q, r, bot], ss.at[2], rs.at[2], right)
        dsl[q, pos, top, :] = mine(q, pos, 0, 128, hl).astype(BF16)
        send(dsl.at[q, pos, top], drr.at[q, r, top], ss.at[3], rs.at[3], left)
        oacc[q, pos] = mine(q, pos, 0, 256, h).reshape(4, 64, 256)

    def pass_right(q, pos):
        r = order[pos]
        ss, rs = d_s.at[q, pos], d_r.at[q, r]
        got(dfl.at[q, r], ss.at[0], rs.at[0])
        dsr[q, pos, top, :] = (mine(q, pos, 0, 128, hr) + dfl[q, r].astype(F32)).astype(BF16)
        send(dsr.at[q, pos, top], drl.at[q, r, top], ss.at[4], rs.at[4], right)

    def pass_left(q, pos):
        r = order[pos]
        ss, rs = d_s.at[q, pos], d_r.at[q, r]
        got(dfr.at[q, r], ss.at[1], rs.at[1])
        dsl[q, pos, bot, :] = (mine(q, pos, 128, 128, hl) + dfr[q, r].astype(F32)).astype(BF16)
        send(dsl.at[q, pos, bot], drr.at[q, r, bot], ss.at[5], rs.at[5], left)

    writes = []

    def finish(q, pos):
        r = order[pos]
        for i, ref in (
            (2, drl.at[q, r, bot]), (3, drr.at[q, r, top]), (4, drl.at[q, r, top]), (5, drr.at[q, r, bot])
        ):
            got(ref, d_s.at[q, pos, i], d_r.at[q, r, i])
        gathered = drl[q, r].astype(F32) + drr[q, r].astype(F32)
        oacc[q, pos] = oacc[q, pos] + gathered.reshape(4, 64, 256)
        w = pltpu.make_async_copy(oacc.at[q, pos], out.at[r, :, q], o_s.at[q, pos])
        w.start()
        writes.append(w)

    temporal_out(0)
    w_start()
    temporal_out(1)
    row = lax.broadcasted_iota(jnp.int32, (256, 256), 0)
    col = lax.broadcasted_iota(jnp.int32, (256, 256), 1)
    bias[...] = jnp.where((row % 16 == col % 16) & (row // 16 >= col // 16), 0.0, -1e30)
    loads[0].wait()
    temporal_in(0)
    proj_far(0)
    proj_near(0)
    loads[4].wait()
    proj_own(0)
    proj_pass(0)
    w_forward()
    temporal_in(1)
    proj_far(1)
    norm_one(0)
    proj_near(1)
    w_in(0)
    swap_in(0)
    qkv(0, 0)
    w_in(1)
    qkv(0, 1)
    w_in(2)
    qkv(0, 2)
    w_in(3)
    qkv(0, 3)
    proj_own(1)
    proj_pass(1)
    loads[5].wait()
    ag_wo = (wo, wo_s, wo_r)
    ag_start(*ag_wo)
    attend(0, 0)
    attend(0, 1)
    norm_one(1)
    ag_forward(*ag_wo)
    attend(0, 2)
    attend(0, 3)
    swap_in(1)
    qkv(1, 0)
    qkv(1, 1)
    for pos in (1, 2, 3):
        ag_wait(*ag_wo, pos)
    out_proj(0)
    qkv(1, 2)
    qkv(1, 3)
    loads[2].wait()
    loads[3].wait()
    mlp(0, 0)
    attend(1, 0)
    ag_forward(*ag_two(0))
    attend(1, 1)
    attend(1, 2)
    mlp(0, 1)
    attend(1, 3)
    mlp(0, 2)
    pass_right(0, 1)
    pass_left(0, 2)
    mlp(0, 3)
    out_proj(1)
    mlp(1, 0)
    pass_right(0, 3)
    pass_left(0, 0)
    pass_right(0, 0)
    pass_left(0, 3)
    pass_right(0, 2)
    pass_left(0, 1)
    ag_forward(*ag_two(1))
    mlp(1, 1)
    mlp(1, 2)
    pass_right(1, 1)
    pass_left(1, 2)
    for pos in (1, 2, 0, 3):
        finish(0, pos)
    mlp(1, 3)
    pass_right(1, 3)
    pass_left(1, 0)
    pass_right(1, 0)
    pass_left(1, 3)
    pass_right(1, 2)
    pass_left(1, 1)
    for pos in (1, 2, 0, 3):
        finish(1, pos)

    for s in sends:
        s.wait_send()
    for q in range(2):
        for r in range(4):
            block = qs.at[q, r, pl.ds(0, 240)]
            rc(block, block, a_s.at[q, r], a_r.at[q, r], right).wait_send()

    @pl.when(home)
    def _():
        for i in range(6):
            w_copy(i).wait_send()
        for pos in range(4):
            w_share(pos).wait_send()
        for q in range(2):
            for r in range(4):
                block = att_s.at[q, r, pl.ds(0, 15)]
                rc(block, block, b_s.at[q, r], b_r.at[q, r], right).wait_send()

    @pl.when(jnp.logical_not(home))
    def _():
        for q in range(2):
            swap(q).wait_send()
            for r in range(4):
                block = att_s.at[q, r]
                rc(block, block, b_s.at[q, r], b_r.at[q, r], right).wait_send()

    for w in writes:
        w.wait()


def body(temporal, frame_ids, proj_weight, embed_table, qkv_weight, out_weight, gate_up, down_weight, norm_gains):
    c = lax.axis_index("codebook")
    h = lax.axis_index("hidden")
    start_id = embed_table.shape[1] - 1
    own_ids = lax.dynamic_slice_in_dim(frame_ids[:, 0], h * 512, 512, 0)
    own_ids = own_ids.reshape(4, 2, 64).transpose(1, 0, 2).reshape(512)
    earlier = lax.ppermute(own_ids, "codebook", [(i, i + 1) for i in range(15)])
    previous = jnp.where(c == 0, start_id, earlier)
    emb = embed_table[0][previous].reshape(2, 256, 1024)
    vm, dma = pltpu.VMEM, pltpu.SemaphoreType.DMA
    any_spec = pl.BlockSpec(memory_space=pl.ANY)
    result = pl.pallas_call(
        kernel,
        name="depth_layer",
        out_shape=jax.ShapeDtypeStruct((4, 4, 2, 64, 256), F32),
        in_specs=[any_spec] * 7 + [pl.BlockSpec(memory_space=pltpu.VMEM)],
        out_specs=any_spec,
        scratch_shapes=[
            vm((2, 16, 64, 1024), BF16), vm((1024, 1024), BF16), vm((4, 3, 1024, 256), BF16), vm((4, 256, 1024), BF16),
            vm((2, 1024, 1024), BF16), vm((1024, 1024), BF16), vm((2, 256, 1024), BF16),
            vm((2, 256, 1024), BF16), vm((2, 256, 1024), BF16), vm((2, 256, 1024), BF16),
            vm((2, 128, 1024), BF16), vm((2, 128, 1024), BF16), vm((2, 256, 1024), BF16), vm((2, 256, 1024), BF16),
            vm((2, 256, 1024), F32),
            vm((2, 256, 1024), BF16), vm((2, 256, 1024), BF16), vm((2, 4, 256, 768), BF16), vm((2, 4, 16, 16, 768), BF16),
            vm((2, 4, 16, 16, 256), BF16), vm((2, 4, 256, 256), BF16), vm((256, 256), F32),
            vm((2, 4, 256, 1024), BF16), vm((2, 4, 256, 1024), BF16),
            vm((2, 4, 256, 256), BF16), vm((2, 4, 256, 256), BF16), vm((2, 4, 256, 256), BF16),
            vm((2, 4, 128, 256), BF16), vm((2, 4, 128, 256), BF16),
            vm((2, 4, 256, 256), BF16), vm((2, 4, 256, 256), BF16),
            vm((2, 4, 4, 64, 256), F32),
            dma((8,)), dma((2, 15)), dma((2, 16)), dma((6,)), dma((6,)), dma((2, 6)), dma((2, 6)),
            dma((6,)), dma((6,)), dma((4,)), dma((4,)), dma((2,)), dma((2,)), dma((2, 6)), dma((2, 6)), dma((2, 4)), dma((2, 4)), dma((2, 4)), dma((2, 4)),
            dma((2, 4, 6)), dma((2, 4, 6)), dma((2, 4)),
        ],
        compiler_params=pltpu.CompilerParams(
            collective_id=0, has_side_effects=True, vmem_limit_bytes=67043328
        ),
    )(
        temporal.reshape(2, 64, 1024), emb, proj_weight, qkv_weight, out_weight, gate_up, down_weight, norm_gains
    )
    return result.reshape(1, 2048, 256)


def solution(mesh):
    placed = (
        P(("frames", "codebook"), "hidden"),
        P("frames", "codebook"),
        P("codebook", "hidden", None),
        P("codebook", None, None),
        P("codebook", None, None, "hidden"),
        P("codebook", "hidden", None),
        P("codebook", None, None, "hidden"),
        P("codebook", "hidden", None),
        P("codebook", None, None),
    )
    return jax.shard_map(
        body,
        mesh=mesh,
        in_specs=placed,
        out_specs=P("codebook", "frames", "hidden"),
        check_vma=False,
    )
```

```python
import functools

import jax
import jax.numpy as jnp
from jax import lax
from jax.experimental import pallas as pl
from jax.experimental.pallas import tpu as pltpu
from jax.sharding import PartitionSpec as P

HEADS = 16
MESH = pl.DeviceIdType.MESH
F32 = jnp.float32
BF16 = jnp.bfloat16
PLANE = (
    (1, 0, 2), (0, 1, 2), (1, 0, 1), (1, 0, 3), (1, 1, 2), (0, 0, 2), (0, 1, 1), (0, 1, 3),
    (1, 0, 0), (1, 1, 1), (1, 1, 3), (0, 0, 1), (0, 0, 3), (0, 1, 0), (1, 1, 0),
)
ROW = (1, 3, 2)


def kernel(
    temporal, ids_in, table_in, wp_in, wqkv_in, wo_in, wgu_in, wd_in, gains, out,
    tbuf, wp, wq, wo, wgu, wd, emb, first, ids_own, ids, spread, hot,
    ps2, psr, psl, pfl, pfr, prl, prr, x0,
    own_s, own_r, nq, qs, qr, att_s, att_r, bias, gain,
    n2, act, ds2, dsr, dsl, dfl, dfr, drl, drr, dos, dor, oacc,
    loc, i_s, i_r, t_s, t_r, wo_s, wo_r, p_s, p_r, w_s, w_r, v_s, v_r, u_s, u_r, g_s, g_r, e_s, e_r, x_s, x_r, m_s, m_r, a_s, a_r, b_s, b_r, d_s, d_r, o_s, gate,
):
    f = lax.axis_index("frames")
    c = lax.axis_index("codebook")
    h = lax.axis_index("hidden")
    hr, hl, ho = (h + 1) % 4, (h + 3) % 4, (h + 2) % 4
    right, left = (f, c, hr), (f, c, hl)
    y, x, k = c // 8, (c // 2) % 4, c % 2
    order = (h, hl, hr, ho)
    top, bot = pl.ds(0, 128), pl.ds(128, 128)
    sends = []

    def rc(src, dst, ss, rs, dev):
        return pltpu.make_async_remote_copy(
            src_ref=src, dst_ref=dst, send_sem=ss, recv_sem=rs, device_id=dev, device_id_type=MESH
        )

    def send(src, dst, ss, rs, dev):
        s = rc(src, dst, ss, rs, dev)
        s.start()
        sends.append(s)

    def got(ref, ss, rs):
        rc(ref, ref, ss, rs, right).wait_recv()

    loads = [
        pltpu.make_async_copy(s, d, loc.at[i])
        for i, (s, d) in enumerate((
            (wp_in.at[0], wp), (wqkv_in.at[0], wq.at[h]), (wgu_in.at[0], wgu), (wd_in.at[0], wd), (ids_in.at[h], ids_own),
            (wo_in.at[0], wo.at[h]), (temporal.at[0], tbuf.at[0, c]), (temporal.at[1], tbuf.at[1, c]),
            (table_in.at[0, pl.ds(0, 2048)], act), (table_in.at[0, pl.ds(2048, 1)], first),
        ))
    ]
    home = k == f
    away = jnp.logical_not(home)
    worker = f * 8 + y * 4 + x
    book = c - k + f
    partner = (f, c + 1 - 2 * k, h)
    owner = lambda at: (k, book, at)
    for i in (4, 6, 7, 0):
        loads[i].start()

    @pl.when(home)
    def _():
        for i in (1, 9, 8, 5, 2, 3):
            loads[i].start()

    barrier = pltpu.get_barrier_semaphore()

    def greet(n, carry):
        pl.semaphore_signal(
            barrier, inc=1, device_id=((f + n // 16) % 2, (c + n % 16) % 16, h), device_id_type=MESH
        )
        return carry

    pl.semaphore_signal(barrier, inc=1, device_id=right, device_id_type=MESH)
    pl.semaphore_signal(barrier, inc=1, device_id=left, device_id_type=MESH)
    for at in (hr, hl):
        pl.semaphore_signal(barrier, inc=1, device_id=(1 - f, c + 1 - 2 * k, at), device_id_type=MESH)
    lax.fori_loop(1, 32, greet, 0)
    pl.semaphore_wait(barrier, 35)

    common = (
        (table_in.at[0, pl.ds(2048, 1)], first, 9), (table_in.at[0, pl.ds(0, 2048)], act, 8),
        (gains.at[0], gain, None), (wgu_in.at[0], wgu, 2), (wd_in.at[0], wd, 3),
    )

    def share(i):
        return rc(common[i][0], common[i][1], g_s.at[i], g_r.at[i], partner)

    def share_out():
        @pl.when(home)
        def _():
            gain[...] = gains[0]
            for i in range(5):
                share(i).start()

    def ready(i):
        @pl.when(home)
        def _():
            if common[i][2] is not None:
                loads[common[i][2]].wait()

        @pl.when(away)
        def _():
            share(i).wait_recv()

    def ids_out():
        loads[4].wait()
        send(ids_own, ids, i_s.at[0], i_r.at[0], ((c + 1) % 2, ((c + 1) % 16) // 2 * 2 + f, h))

    def ids_spread():
        got(ids, i_s.at[0], i_r.at[0])
        for s in range(4):
            turned = jnp.transpose(jnp.broadcast_to(ids[s:s + 1, :].astype(F32), (128, 128))).astype(jnp.int32)
            for q in range(2):
                spread[q, s * 64:s * 64 + 64, :] = turned[q * 64:q * 64 + 64]

    def embed(q):
        @pl.when(book == 0)
        def _():
            emb[q] = jnp.broadcast_to(first[...], (256, 1024))

        @pl.when(book != 0)
        def _():
            lane = lax.broadcasted_iota(jnp.int32, (256, 128), 1)
            for b in range(16):
                hot[:, b * 128:(b + 1) * 128] = jnp.where(spread[q] == lane + b * 128, 1.0, 0.0).astype(BF16)

            def tile(n, carry):
                cols = pl.ds(pl.multiple_of(n * 256, 256), 256)
                emb[q, :, cols] = jnp.dot(hot[...], act[:, cols], preferred_element_type=F32).astype(BF16)
                return carry

            lax.fori_loop(0, 4, tile, 0)

    def core_of(oy, ox, core):
        return ((y + oy) % 2) * 8 + ((x + ox) % 4) * 2 + core

    def temporal_move(q, src, i, dev):
        send(tbuf.at[q, src], tbuf.at[q, src], t_s.at[q, i], t_r.at[q, src], dev)

    def temporal_out(q):
        loads[6 + q].wait()
        temporal_move(q, c, 0, (f, core_of(1, 0, k), h))
        for i, ox in enumerate(ROW):
            temporal_move(q, c, 1 + i, (f, core_of(0, ox, k), h))
        temporal_move(q, c, 4, partner)

    def temporal_pass(q):
        across = core_of(1, 0, k)
        got(tbuf.at[q, across], t_s.at[q, 0], t_r.at[q, across])
        for i, ox in enumerate(ROW):
            temporal_move(q, across, 5 + i, (f, core_of(0, ox, k), h))
        temporal_move(q, across, 8, partner)

    def temporal_in(q):
        for oy in range(2):
            for i, ox in enumerate(ROW):
                src = core_of(oy, 4 - ox, k)
                got(tbuf.at[q, src], t_s.at[q, 0], t_r.at[q, src])
                temporal_move(q, src, 9 + oy * 3 + i, partner)
        for oy in range(2):
            for ox in range(4):
                src = core_of(oy, ox, 1 - k)
                got(tbuf.at[q, src], t_s.at[q, 0], t_r.at[q, src])

    def proj(q, block, row0, rows, store):
        def tile(n, carry):
            cols = pl.ds(pl.multiple_of(n * 256, 256), 256)
            lhs = tbuf[q, pl.ds(block * 4 + row0 // 64, rows // 64)].reshape(rows, 1024)
            store(cols, jnp.dot(lhs, wp[:, cols], preferred_element_type=F32))
            return carry

        lax.fori_loop(0, 4, tile, 0)

    def into(ref, row0, rows, extra=None):
        def store(cols, value):
            if extra is not None:
                value = value + extra[:, cols].astype(F32)
            ref[pl.ds(row0, rows), cols] = value.astype(ref.dtype)

        return store

    def proj_far(q):
        ss, rs = p_s.at[q], p_r.at[q]
        proj(q, ho, 0, 256, into(ps2.at[q], 0, 256))
        send(ps2.at[q, top], pfl.at[q], ss.at[0], rs.at[0], right)
        send(ps2.at[q, bot], pfr.at[q], ss.at[1], rs.at[1], left)

    def proj_near(q):
        ss, rs = p_s.at[q], p_r.at[q]
        proj(q, hr, 128, 128, into(psr.at[q], 128, 128))
        send(psr.at[q, bot], prl.at[q, bot], ss.at[2], rs.at[2], right)
        proj(q, hl, 0, 128, into(psl.at[q], 0, 128))
        send(psl.at[q, top], prr.at[q, top], ss.at[3], rs.at[3], left)

    def own_copy(q):
        return rc(own_s.at[q], own_r.at[q], x_s.at[q], x_r.at[q], owner(h))

    def proj_own(q):
        proj(q, h, 0, 256, into(x0.at[q], 0, 256))

    def near_in(q):
        got(prl.at[q, bot], p_s.at[q, 2], p_r.at[q, 2])
        got(prr.at[q, top], p_s.at[q, 3], p_r.at[q, 3])

    def own_send(q):
        @pl.when(away)
        def _():
            near_in(q)
            for half, near in ((top, prr), (bot, prl)):
                own_s[q, half, :] = (x0[q, half, :] + near[q, half, :].astype(F32)).astype(BF16)
            own_copy(q).start()

    def proj_pass(q):
        ss, rs = p_s.at[q], p_r.at[q]
        got(pfl.at[q], ss.at[0], rs.at[0])
        proj(q, hr, 0, 128, into(psr.at[q], 0, 128, pfl.at[q]))
        send(psr.at[q, top], prl.at[q, top], ss.at[4], rs.at[4], owner(hr))
        got(pfr.at[q], ss.at[1], rs.at[1])
        proj(q, hl, 128, 128, into(psl.at[q], 128, 128, pfr.at[q]))
        send(psl.at[q, bot], prr.at[q, bot], ss.at[5], rs.at[5], owner(hl))

    def norm_rows(q, dst, scale_by, base, extras, first_row=0, last_row=256):
        def chunk(n, carry):
            rows = pl.ds(pl.multiple_of(first_row + n * 32, 32), 32)
            v = base[q, rows, :].astype(F32)
            for e in extras:
                v = v + e[q, rows, :].astype(F32)
            if extras:
                x0[q, rows, :] = v
            scale = lax.rsqrt(jnp.mean(v * v, axis=-1, keepdims=True) + 1e-05)
            dst[rows, :] = (v * scale * scale_by).astype(BF16)
            return carry

        lax.fori_loop(0, (last_row - first_row) // 32, chunk, 0)

    def norm_one(q):
        got(prl.at[q, top], p_s.at[q, 4], p_r.at[q, 4])
        got(prr.at[q, bot], p_s.at[q, 5], p_r.at[q, 5])

        @pl.when(home)
        def _():
            near_in(q)
            norm_rows(q, nq.at[q], gain[0:1, :], x0, (prl, prr, emb))

        @pl.when(away)
        def _():
            own_copy(q).wait_recv()
            norm_rows(q, nq.at[q], gain[0:1, :], own_r, (prl, emb), 0, 128)
            norm_rows(q, nq.at[q], gain[0:1, :], own_r, (prr, emb), 128, 256)

    def together(q):
        @pl.when(away)
        def _():
            pl.semaphore_signal(gate.at[q], inc=1, device_id=partner, device_id_type=MESH)

        @pl.when(home)
        def _():
            pl.semaphore_wait(gate.at[q], 1)

    def ag_start(buf, ss, rs):
        send(buf.at[h, top], buf.at[h, top], ss.at[0], rs.at[0], right)
        send(buf.at[h, bot], buf.at[h, bot], ss.at[2], rs.at[2], left)
        send(buf.at[h, bot], buf.at[h, bot], ss.at[1], rs.at[1], right)
        send(buf.at[h, top], buf.at[h, top], ss.at[3], rs.at[3], left)

    def ag_forward(buf, ss, rs):
        got(buf.at[hl, top], ss.at[0], rs.at[0])
        send(buf.at[hl, top], buf.at[hl, top], ss.at[4], rs.at[4], right)
        got(buf.at[hr, bot], ss.at[2], rs.at[2])
        send(buf.at[hr, bot], buf.at[hr, bot], ss.at[5], rs.at[5], left)

    def ag_wait(buf, ss, rs, pos):
        if pos == 1:
            got(buf.at[hl, bot], ss.at[1], rs.at[1])
        if pos == 2:
            got(buf.at[hr, top], ss.at[3], rs.at[3])
        if pos == 3:
            got(buf.at[ho, top], ss.at[4], rs.at[4])
            got(buf.at[ho, bot], ss.at[5], rs.at[5])

    ag_two = lambda q: (n2.at[q], m_s.at[q], m_r.at[q])

    class Gathered:
        def __init__(self, part, halves, load, ss, rs, vs, vr):
            self.part, self.halves, self.load = part, halves, load
            self.sems = (ss, rs, vs, vr)

        def copy(self, i):
            low, high = self.halves
            at, rows, dev = ((h, low, right), (h, high, right), (h, high, left), (h, low, left),
                             (hl, low, right), (hr, high, left))[i]
            block = self.part(at, rows)
            return rc(block, block, self.sems[0].at[i], self.sems[1].at[i], dev)

        def arrive(self, i):
            low, high = self.halves
            at, rows = ((hl, low), (hl, high), (hr, high), (hr, low), (ho, low), (ho, high))[i]
            got(self.part(at, rows), self.sems[0].at[i], self.sems[1].at[i])

        def give(self, pos):
            block = self.part(order[pos], None)
            return rc(block, block, self.sems[2].at[pos], self.sems[3].at[pos], partner)

        def start(self):
            @pl.when(home)
            def _():
                loads[self.load].wait()
                for i in (0, 2, 1, 3):
                    self.copy(i).start()
                self.give(0).start()

        def forward(self):
            @pl.when(home)
            def _():
                self.arrive(0)
                self.copy(4).start()
                self.arrive(2)
                self.copy(5).start()

        def take(self, pos):
            @pl.when(home)
            def _():
                for i in ((), (1,), (3,), (4, 5))[pos]:
                    self.arrive(i)
                if pos:
                    self.give(pos).start()

            @pl.when(away)
            def _():
                self.give(pos).wait_recv()

        def drain(self):
            for i in range(6):
                self.copy(i).wait_send()
            for pos in range(4):
                self.give(pos).wait_send()

    w_qkv = Gathered(
        lambda at, rows: wq.at[at] if rows is None else wq.at[at, :, rows],
        (pl.ds(0, 512), pl.ds(512, 512)), 1, w_s, w_r, v_s, v_r,
    )
    w_out = Gathered(
        lambda at, rows: wo.at[at] if rows is None else wo.at[at, rows], (top, bot), 5, wo_s, wo_r, u_s, u_r
    )

    def qkv(q, pos):
        r = order[pos]
        for i in range(3):
            part = jnp.dot(nq[q], wq[r, i], preferred_element_type=F32)
            qs[q, r, :, i * 256:(i + 1) * 256] = part.astype(BF16)

        for of, oy, ox in PLANE:
            df, dy, dx = (f + of) % 2, (y + oy) % 2, (x + ox) % 4
            rc(
                qs.at[q, r, pl.ds((df * 8 + dy * 4 + dx) * 16, 16)], qr.at[q, r, book],
                a_s.at[q, r], a_r.at[q, r], (df, dy * 8 + dx * 2 + k, h),
            ).start()
        qr[q, r, book] = qs[q, r, pl.ds(pl.multiple_of(worker * 16, 16), 16), :]

    def attend(q, pos):
        r = order[pos]
        got(qr.at[q, r, pl.ds(0, 15)], a_s.at[q, r], a_r.at[q, r])

        def unit(n, carry):
            pair = n * 128
            take = lambda i: qr[
                q, r, :, :, pl.ds(pl.multiple_of(i * 256 + pair, 128), 128)
            ].reshape(256, 128)
            qq, kk, v = take(0), take(1), take(2)
            lane = lax.broadcasted_iota(jnp.int32, (256, 128), 1)
            halves = []
            for half in range(2):
                mine = (lane // 64) == half
                qh = jnp.where(mine, qq, jnp.zeros_like(qq))
                parts = []
                for rows, width in ((slice(0, 128), 128), (slice(128, 256), 256)):
                    s = lax.dot_general(
                        qh[rows], kk[:width], (((1,), (1,)), ((), ())), preferred_element_type=F32
                    )
                    s = s * 0.125 + bias[rows, :width]
                    e = jnp.exp(s - jnp.max(s, axis=-1, keepdims=True))
                    total = jnp.sum(e, axis=-1, keepdims=True)
                    o = jnp.dot(e.astype(BF16), v[:width], preferred_element_type=F32)
                    parts.append(o / total)
                halves.append(jnp.concatenate(parts, axis=0))
            o = jnp.where((lane // 64) == 0, halves[0], halves[1]).astype(BF16)
            att_s[q, r, :, :, pl.ds(pl.multiple_of(pair, 128), 128)] = o.reshape(16, 16, 128)
            return carry

        lax.fori_loop(0, 2, unit, 0)

        for of, oy, ox in PLANE:
            df, dy, dx = (f + of) % 2, (y + oy) % 2, (x + ox) % 4
            rc(
                att_s.at[q, r, dy * 8 + dx * 2 + df], att_r.at[q, r, pl.ds(worker * 16, 16)],
                b_s.at[q, r], b_r.at[q, r], (df, dy * 8 + dx * 2 + k, h),
            ).start()
        att_r[q, r, pl.ds(pl.multiple_of(worker * 16, 16), 16), :] = att_s[q, r, book]

    def out_proj(q):
        for src in order:
            got(att_r.at[q, src, pl.ds(0, 240)], b_s.at[q, src], b_r.at[q, src])

        def tile(n, carry):
            cols = pl.ds(pl.multiple_of(n * 256, 256), 256)
            total = x0[q, :, cols]
            for src in range(4):
                total = total + jnp.dot(att_r[q, src], wo[src, :, cols], preferred_element_type=F32)
            x0[q, :, cols] = total
            return carry

        lax.fori_loop(0, 4, tile, 0)
        norm_rows(q, n2.at[q, h], gain[1:2, :], x0, ())
        ag_start(*ag_two(q))

    def mine(q, pos, row0, rows, target):
        cols = pl.ds(pl.multiple_of(target * 256, 256), 256)
        value = jnp.dot(act[pl.ds((q * 4 + pos) * 256 + row0, rows), :], wd[:, cols], preferred_element_type=F32)
        if pos == 0:
            value = value + x0[q, pl.ds(row0, rows), cols]
        return value

    to_right = lambda q: owner(hr) if q else right
    to_left = lambda q: owner(hl) if q else left

    def last_copy(q, pos):
        r = order[pos]
        return rc(dos.at[q, pos], dor.at[q, r], e_s.at[q, pos], e_r.at[q, r], owner(h))

    def mlp(q, pos):
        r = order[pos]
        ss, rs = d_s.at[q, pos], d_r.at[q, r]
        ag_wait(*ag_two(q), pos)

        def tile(n, carry):
            cols = pl.ds(pl.multiple_of(n * 256, 256), 256)
            g = jnp.dot(n2[q, r], wgu[0, :, cols], preferred_element_type=F32)
            u = jnp.dot(n2[q, r], wgu[1, :, cols], preferred_element_type=F32)
            act[pl.ds((q * 4 + pos) * 256, 256), cols] = (g / (1.0 + jnp.exp(-g)) * u).astype(BF16)
            return carry

        lax.fori_loop(0, 4, tile, 0)
        ds2[q, pos] = mine(q, pos, 0, 256, ho).astype(BF16)
        send(ds2.at[q, pos, top], dfl.at[q, r], ss.at[0], rs.at[0], right)
        send(ds2.at[q, pos, bot], dfr.at[q, r], ss.at[1], rs.at[1], left)
        dsr[q, pos, bot, :] = mine(q, pos, 128, 128, hr).astype(BF16)
        send(dsr.at[q, pos, bot], drl.at[q, r, bot], ss.at[2], rs.at[2], to_right(q))
        dsl[q, pos, top, :] = mine(q, pos, 0, 128, hl).astype(BF16)
        send(dsl.at[q, pos, top], drr.at[q, r, top], ss.at[3], rs.at[3], to_left(q))
        if q == 0:
            oacc[q, pos] = mine(q, pos, 0, 256, h).reshape(4, 64, 256)
            return

        @pl.when(home)
        def _():
            oacc[q, pos] = mine(q, pos, 0, 256, h).reshape(4, 64, 256)

        @pl.when(away)
        def _():
            dos[q, pos] = mine(q, pos, 0, 256, h).astype(BF16)
            last_copy(q, pos).start()

    def pass_right(q, pos):
        r = order[pos]
        ss, rs = d_s.at[q, pos], d_r.at[q, r]
        got(dfl.at[q, r], ss.at[0], rs.at[0])
        dsr[q, pos, top, :] = (mine(q, pos, 0, 128, hr) + dfl[q, r].astype(F32)).astype(BF16)
        send(dsr.at[q, pos, top], drl.at[q, r, top], ss.at[4], rs.at[4], to_right(q))

    def pass_left(q, pos):
        r = order[pos]
        ss, rs = d_s.at[q, pos], d_r.at[q, r]
        got(dfr.at[q, r], ss.at[1], rs.at[1])
        dsl[q, pos, bot, :] = (mine(q, pos, 128, 128, hl) + dfr[q, r].astype(F32)).astype(BF16)
        send(dsl.at[q, pos, bot], drr.at[q, r, bot], ss.at[5], rs.at[5], to_left(q))

    def write(q, pos):
        return pltpu.make_async_copy(oacc.at[q, pos], out.at[order[pos], :, q], o_s.at[q, pos])

    def finish(q, pos):
        r = order[pos]
        for i, ref in (
            (2, drl.at[q, r, bot]), (3, drr.at[q, r, top]), (4, drl.at[q, r, top]), (5, drr.at[q, r, bot])
        ):
            got(ref, d_s.at[q, pos, i], d_r.at[q, r, i])
        gathered = drl[q, r].astype(F32) + drr[q, r].astype(F32)

        @pl.when(home)
        def _():
            oacc[q, pos] = oacc[q, pos] + gathered.reshape(4, 64, 256)
            write(q, pos).start()

        @pl.when(away)
        def _():
            if q == 0:
                dos[q, pos] = (oacc[q, pos].reshape(256, 256) + gathered).astype(BF16)
                last_copy(q, pos).start()
            else:
                last_copy(q, pos).wait_recv()
                oacc[q, pos] = (dor[q, r].astype(F32) + gathered).reshape(4, 64, 256)
                write(q, pos).start()

    def land(q, pos):
        @pl.when(away)
        def _():
            last_copy(q, pos).wait_recv()
            oacc[q, pos] = dor[q, order[pos]].astype(F32).reshape(4, 64, 256)
            write(q, pos).start()

    ids_out()
    temporal_out(0)
    w_qkv.start()
    share_out()
    row = lax.broadcasted_iota(jnp.int32, (256, 256), 0)
    col = lax.broadcasted_iota(jnp.int32, (256, 256), 1)
    bias[...] = jnp.where((row % 16 == col % 16) & (row // 16 >= col // 16), 0.0, -1e30)
    temporal_pass(0)
    temporal_out(1)
    ids_spread()
    loads[0].wait()
    temporal_in(0)
    temporal_pass(1)
    proj_far(0)
    proj_near(0)
    proj_own(0)
    ready(0)
    ready(1)
    embed(0)
    proj_pass(0)
    temporal_in(1)
    proj_far(1)
    w_qkv.forward()
    own_send(0)
    for pos in range(3):
        w_qkv.take(pos)
    embed(1)
    ready(2)
    norm_one(0)
    proj_near(1)
    qkv(0, 0)
    qkv(0, 1)
    qkv(0, 2)
    w_qkv.take(3)
    qkv(0, 3)
    w_out.start()
    proj_own(1)
    attend(0, 0)
    attend(0, 1)
    w_out.forward()
    attend(0, 2)
    attend(0, 3)
    proj_pass(1)
    own_send(1)
    for pos in range(4):
        w_out.take(pos)
    out_proj(0)
    ready(3)
    ready(4)
    mlp(0, 0)
    norm_one(1)
    together(1)
    qkv(1, 0)
    ag_forward(*ag_two(0))
    qkv(1, 1)
    qkv(1, 2)
    qkv(1, 3)
    mlp(0, 1)
    mlp(0, 2)
    pass_right(0, 1)
    pass_left(0, 2)
    attend(1, 0)
    attend(1, 1)
    mlp(0, 3)
    attend(1, 2)
    attend(1, 3)
    pass_right(0, 3)
    pass_left(0, 0)
    pass_right(0, 0)
    pass_left(0, 3)
    pass_right(0, 2)
    pass_left(0, 1)
    out_proj(1)
    mlp(1, 0)
    for pos in (1, 2, 0, 3):
        finish(0, pos)
    ag_forward(*ag_two(1))
    mlp(1, 1)
    mlp(1, 2)
    pass_right(1, 1)
    pass_left(1, 2)
    for pos in range(4):
        land(0, pos)
    mlp(1, 3)
    pass_right(1, 3)
    pass_left(1, 0)
    pass_right(1, 0)
    pass_left(1, 3)
    pass_right(1, 2)
    pass_left(1, 1)
    for pos in (1, 2, 0, 3):
        finish(1, pos)

    for s in sends:
        s.wait_send()
    for q in range(2):
        for r in range(4):
            block = qs.at[q, r, pl.ds(0, 240)]
            rc(block, block, a_s.at[q, r], a_r.at[q, r], right).wait_send()
            block = att_s.at[q, r, pl.ds(0, 15)]
            rc(block, block, b_s.at[q, r], b_r.at[q, r], right).wait_send()

    @pl.when(home)
    def _():
        w_qkv.drain()
        w_out.drain()
        for i in range(5):
            share(i).wait_send()

    @pl.when(away)
    def _():
        for q in range(2):
            own_copy(q).wait_send()
            for pos in range(4):
                last_copy(q, pos).wait_send()

    for q in range(2):
        for pos in range(4):
            write(q, pos).wait()


def body(temporal, frame_ids, proj_weight, embed_table, qkv_weight, out_weight, gate_up, down_weight, norm_gains):
    vm, dma = pltpu.VMEM, pltpu.SemaphoreType.DMA
    any_spec = pl.BlockSpec(memory_space=pl.ANY)
    result = pl.pallas_call(
        kernel,
        name="depth_layer",
        out_shape=jax.ShapeDtypeStruct((4, 4, 2, 64, 256), F32),
        in_specs=[any_spec] * 8 + [pl.BlockSpec(memory_space=pltpu.VMEM)],
        out_specs=any_spec,
        scratch_shapes=[
            vm((2, 16, 64, 1024), BF16), vm((1024, 1024), BF16), vm((4, 3, 1024, 256), BF16), vm((4, 256, 1024), BF16),
            vm((2, 1024, 1024), BF16), vm((1024, 1024), BF16), vm((2, 256, 1024), BF16),
            vm((1, 1024), BF16), vm((4, 128), jnp.int32), vm((4, 128), jnp.int32),
            vm((2, 256, 128), jnp.int32), vm((256, 2048), BF16),
            vm((2, 256, 1024), BF16), vm((2, 256, 1024), BF16), vm((2, 256, 1024), BF16),
            vm((2, 128, 1024), BF16), vm((2, 128, 1024), BF16), vm((2, 256, 1024), BF16), vm((2, 256, 1024), BF16),
            vm((2, 256, 1024), F32),
            vm((2, 256, 1024), BF16), vm((2, 256, 1024), BF16), vm((2, 256, 1024), BF16), vm((2, 4, 256, 768), BF16), vm((2, 4, 16, 16, 768), BF16),
            vm((2, 4, 16, 16, 256), BF16), vm((2, 4, 256, 256), BF16), vm((256, 256), F32), vm((2, 1024), F32),
            vm((2, 4, 256, 1024), BF16), vm((2048, 1024), BF16),
            vm((2, 4, 256, 256), BF16), vm((2, 4, 256, 256), BF16), vm((2, 4, 256, 256), BF16),
            vm((2, 4, 128, 256), BF16), vm((2, 4, 128, 256), BF16),
            vm((2, 4, 256, 256), BF16), vm((2, 4, 256, 256), BF16),
            vm((2, 4, 256, 256), BF16), vm((2, 4, 256, 256), BF16), vm((2, 4, 4, 64, 256), F32),
            dma((10,)), dma((1,)), dma((1,)), dma((2, 15)), dma((2, 16)), dma((6,)), dma((6,)), dma((2, 6)), dma((2, 6)),
            dma((6,)), dma((6,)), dma((4,)), dma((4,)), dma((4,)), dma((4,)), dma((5,)), dma((5,)), dma((2, 4)), dma((2, 4)),
            dma((2,)), dma((2,)), dma((2, 6)), dma((2, 6)), dma((2, 4)), dma((2, 4)), dma((2, 4)), dma((2, 4)),
            dma((2, 4, 6)), dma((2, 4, 6)), dma((2, 4)), pltpu.SemaphoreType.REGULAR((2,)),
        ],
        compiler_params=pltpu.CompilerParams(
            collective_id=0, has_side_effects=True, vmem_limit_bytes=67043328
        ),
    )(
        temporal.reshape(2, 64, 1024), frame_ids.reshape(4, 4, 128), embed_table, proj_weight, qkv_weight, out_weight, gate_up, down_weight, norm_gains
    )
    return result.reshape(1, 2048, 256)


def solution(mesh):
    placed = (
        P(("frames", "codebook"), "hidden"),
        P("frames", "codebook"),
        P("codebook", "hidden", None),
        P("codebook", None, None),
        P("codebook", None, None, "hidden"),
        P("codebook", "hidden", None),
        P("codebook", None, None, "hidden"),
        P("codebook", "hidden", None),
        P("codebook", None, None),
    )
    return jax.shard_map(
        body,
        mesh=mesh,
        in_specs=placed,
        out_specs=P("codebook", "frames", "hidden"),
        check_vma=False,
    )
```

```python
import functools

import jax
import jax.numpy as jnp
from jax import lax
from jax.experimental import pallas as pl
from jax.experimental.pallas import tpu as pltpu
from jax.sharding import PartitionSpec as P

HEADS = 16
MESH = pl.DeviceIdType.MESH
F32 = jnp.float32
BF16 = jnp.bfloat16
PLANE = (
    (1, 0, 2), (0, 1, 2), (1, 0, 1), (1, 0, 3), (1, 1, 2), (0, 0, 2), (0, 1, 1), (0, 1, 3),
    (1, 0, 0), (1, 1, 1), (1, 1, 3), (0, 0, 1), (0, 0, 3), (0, 1, 0), (1, 1, 0),
)
ROW = (1, 3, 2)


def kernel(
    temporal, ids_in, table_in, wp_in, wqkv_in, wo_in, wgu_in, wd_in, gains, out,
    tbuf, wp, wq, wo, wgu, wd, emb, first, ids_own, ids, spread, hot,
    ps2, psr, psl, pfl, pfr, prl, prr, x0,
    own_s, own_r, nq, qs, qr, att_s, att_r, bias, gain,
    n2, act, ds2, dsr, dsl, dfl, dfr, drl, drr, dos, dor, oacc,
    loc, i_s, i_r, t_s, t_r, wo_s, wo_r, p_s, p_r, w_s, w_r, v_s, v_r, u_s, u_r, g_s, g_r, e_s, e_r, x_s, x_r, m_s, m_r, a_s, a_r, b_s, b_r, d_s, d_r, o_s, gate,
):
    f = lax.axis_index("frames")
    c = lax.axis_index("codebook")
    h = lax.axis_index("hidden")
    hr, hl, ho = (h + 1) % 4, (h + 3) % 4, (h + 2) % 4
    right, left = (f, c, hr), (f, c, hl)
    y, x, k = c // 8, (c // 2) % 4, c % 2
    order = (h, hl, hr, ho)
    top, bot = pl.ds(0, 128), pl.ds(128, 128)
    sends = []

    def rc(src, dst, ss, rs, dev):
        return pltpu.make_async_remote_copy(
            src_ref=src, dst_ref=dst, send_sem=ss, recv_sem=rs, device_id=dev, device_id_type=MESH
        )

    def send(src, dst, ss, rs, dev):
        s = rc(src, dst, ss, rs, dev)
        s.start()
        sends.append(s)

    def got(ref, ss, rs):
        rc(ref, ref, ss, rs, right).wait_recv()

    loads = [
        pltpu.make_async_copy(s, d, loc.at[i])
        for i, (s, d) in enumerate((
            (wp_in.at[0], wp), (wqkv_in.at[0], wq.at[h]), (wgu_in.at[0], wgu), (wd_in.at[0], wd), (ids_in.at[h], ids_own),
            (wo_in.at[0], wo.at[h]), (temporal.at[0], tbuf.at[0, c]), (temporal.at[1], tbuf.at[1, c]),
            (table_in.at[0, pl.ds(0, 2048)], act), (table_in.at[0, pl.ds(2048, 1)], first),
        ))
    ]
    home = k == f
    away = jnp.logical_not(home)
    worker = f * 8 + y * 4 + x
    book = c - k + f
    partner = (f, c + 1 - 2 * k, h)
    owner = lambda at: (k, book, at)
    for i in (4, 6, 7, 0):
        loads[i].start()

    @pl.when(home)
    def _():
        for i in (1, 9, 8, 5, 2, 3):
            loads[i].start()

    barrier = pltpu.get_barrier_semaphore()

    def greet(n, carry):
        pl.semaphore_signal(
            barrier, inc=1, device_id=((f + n // 16) % 2, (c + n % 16) % 16, h), device_id_type=MESH
        )
        return carry

    pl.semaphore_signal(barrier, inc=1, device_id=right, device_id_type=MESH)
    pl.semaphore_signal(barrier, inc=1, device_id=left, device_id_type=MESH)
    for at in (hr, hl):
        pl.semaphore_signal(barrier, inc=1, device_id=(1 - f, c + 1 - 2 * k, at), device_id_type=MESH)
    lax.fori_loop(1, 32, greet, 0)
    pl.semaphore_wait(barrier, 35)

    common = (
        (table_in.at[0, pl.ds(2048, 1)], first, 9), (table_in.at[0, pl.ds(0, 2048)], act, 8),
        (gains.at[0], gain, None), (wgu_in.at[0], wgu, 2), (wd_in.at[0], wd, 3),
    )

    def share(i):
        return rc(common[i][0], common[i][1], g_s.at[i], g_r.at[i], partner)

    def share_out(which):
        @pl.when(home)
        def _():
            if 2 in which:
                gain[...] = gains[0]
            for i in which:
                share(i).start()

    def ready(i):
        @pl.when(home)
        def _():
            if common[i][2] is not None:
                loads[common[i][2]].wait()

        @pl.when(away)
        def _():
            share(i).wait_recv()

    def ids_out():
        loads[4].wait()
        send(ids_own, ids, i_s.at[0], i_r.at[0], ((c + 1) % 2, ((c + 1) % 16) // 2 * 2 + f, h))

    def ids_spread():
        got(ids, i_s.at[0], i_r.at[0])
        for s in range(4):
            turned = jnp.transpose(jnp.broadcast_to(ids[s:s + 1, :].astype(F32), (128, 128))).astype(jnp.int32)
            for q in range(2):
                spread[q, s * 64:s * 64 + 64, :] = turned[q * 64:q * 64 + 64]

    def embed(q):
        @pl.when(book == 0)
        def _():
            emb[q] = jnp.broadcast_to(first[...], (256, 1024))

        @pl.when(book != 0)
        def _():
            lane = lax.broadcasted_iota(jnp.int32, (256, 128), 1)
            for b in range(16):
                hot[:, b * 128:(b + 1) * 128] = jnp.where(spread[q] == lane + b * 128, 1.0, 0.0).astype(BF16)

            def tile(n, carry):
                cols = pl.ds(pl.multiple_of(n * 256, 256), 256)
                emb[q, :, cols] = jnp.dot(hot[...], act[:, cols], preferred_element_type=F32).astype(BF16)
                return carry

            lax.fori_loop(0, 4, tile, 0)

    def core_of(oy, ox, core):
        return ((y + oy) % 2) * 8 + ((x + ox) % 4) * 2 + core

    def temporal_move(q, src, i, dev):
        send(tbuf.at[q, src], tbuf.at[q, src], t_s.at[q, i], t_r.at[q, src], dev)

    def temporal_out(q):
        loads[6 + q].wait()
        temporal_move(q, c, 0, (f, core_of(1, 0, k), h))
        for i, ox in enumerate(ROW):
            temporal_move(q, c, 1 + i, (f, core_of(0, ox, k), h))
        temporal_move(q, c, 4, partner)

    def temporal_pass(q):
        across = core_of(1, 0, k)
        got(tbuf.at[q, across], t_s.at[q, 0], t_r.at[q, across])
        for i, ox in enumerate(ROW):
            temporal_move(q, across, 5 + i, (f, core_of(0, ox, k), h))
        temporal_move(q, across, 8, partner)

    def temporal_in(q):
        for oy in range(2):
            for i, ox in enumerate(ROW):
                src = core_of(oy, 4 - ox, k)
                got(tbuf.at[q, src], t_s.at[q, 0], t_r.at[q, src])
                temporal_move(q, src, 9 + oy * 3 + i, partner)
        for oy in range(2):
            for ox in range(4):
                src = core_of(oy, ox, 1 - k)
                got(tbuf.at[q, src], t_s.at[q, 0], t_r.at[q, src])

    def proj(q, block, row0, rows, store):
        def tile(n, carry):
            cols = pl.ds(pl.multiple_of(n * 256, 256), 256)
            lhs = tbuf[q, pl.ds(block * 4 + row0 // 64, rows // 64)].reshape(rows, 1024)
            store(cols, jnp.dot(lhs, wp[:, cols], preferred_element_type=F32))
            return carry

        lax.fori_loop(0, 4, tile, 0)

    def into(ref, row0, rows, extra=None):
        def store(cols, value):
            if extra is not None:
                value = value + extra[:, cols].astype(F32)
            ref[pl.ds(row0, rows), cols] = value.astype(ref.dtype)

        return store

    def proj_far(q):
        ss, rs = p_s.at[q], p_r.at[q]
        proj(q, ho, 0, 256, into(ps2.at[q], 0, 256))
        send(ps2.at[q, top], pfl.at[q], ss.at[0], rs.at[0], right)
        send(ps2.at[q, bot], pfr.at[q], ss.at[1], rs.at[1], left)

    def proj_near(q):
        ss, rs = p_s.at[q], p_r.at[q]
        proj(q, hr, 128, 128, into(psr.at[q], 128, 128))
        send(psr.at[q, bot], prl.at[q, bot], ss.at[2], rs.at[2], right)
        proj(q, hl, 0, 128, into(psl.at[q], 0, 128))
        send(psl.at[q, top], prr.at[q, top], ss.at[3], rs.at[3], left)

    def own_copy(q):
        return rc(own_s.at[q], own_r.at[q], x_s.at[q], x_r.at[q], owner(h))

    def proj_own(q):
        proj(q, h, 0, 256, into(x0.at[q], 0, 256))

    def proj_pass(q):
        ss, rs = p_s.at[q], p_r.at[q]
        got(pfl.at[q], ss.at[0], rs.at[0])
        proj(q, hr, 0, 128, into(psr.at[q], 0, 128, pfl.at[q]))
        send(psr.at[q, top], prl.at[q, top], ss.at[4], rs.at[4], right)
        got(pfr.at[q], ss.at[1], rs.at[1])
        proj(q, hl, 128, 128, into(psl.at[q], 128, 128, pfr.at[q]))
        send(psl.at[q, bot], prr.at[q, bot], ss.at[5], rs.at[5], left)

    def row_chunks(step):
        def chunk(n, carry):
            step(pl.ds(pl.multiple_of(n * 32, 32), 32))
            return carry

        lax.fori_loop(0, 8, chunk, 0)

    def norm_rows(q, dst, scale_by, base, extras):
        def step(rows):
            v = base[q, rows, :].astype(F32)
            for e in extras:
                v = v + e[q, rows, :].astype(F32)
            if extras:
                x0[q, rows, :] = v
            scale = lax.rsqrt(jnp.mean(v * v, axis=-1, keepdims=True) + 1e-05)
            dst[rows, :] = (v * scale * scale_by).astype(BF16)

        row_chunks(step)

    def norm_one(q):
        for i, ref in ((2, prl.at[q, bot]), (3, prr.at[q, top]), (4, prl.at[q, top]), (5, prr.at[q, bot])):
            got(ref, p_s.at[q, i], p_r.at[q, i])

        @pl.when(home)
        def _():
            norm_rows(q, nq.at[q], gain[0:1, :], x0, (prl, prr, emb))

        @pl.when(away)
        def _():
            def step(rows):
                v = x0[q, rows, :] + prl[q, rows, :].astype(F32) + prr[q, rows, :].astype(F32)
                own_s[q, rows, :] = v.astype(BF16)

            row_chunks(step)
            own_copy(q).start()

    def x_in(q):
        @pl.when(away)
        def _():
            own_copy(q).wait_recv()
            norm_rows(q, nq.at[q], gain[0:1, :], own_r, (emb,))

    def together(q):
        @pl.when(away)
        def _():
            pl.semaphore_signal(gate.at[q], inc=1, device_id=partner, device_id_type=MESH)

        @pl.when(home)
        def _():
            pl.semaphore_wait(gate.at[q], 1)

    def ag_start(buf, ss, rs):
        send(buf.at[h, top], buf.at[h, top], ss.at[0], rs.at[0], right)
        send(buf.at[h, bot], buf.at[h, bot], ss.at[2], rs.at[2], left)
        send(buf.at[h, bot], buf.at[h, bot], ss.at[1], rs.at[1], right)
        send(buf.at[h, top], buf.at[h, top], ss.at[3], rs.at[3], left)

    def ag_forward(buf, ss, rs):
        got(buf.at[hl, top], ss.at[0], rs.at[0])
        send(buf.at[hl, top], buf.at[hl, top], ss.at[4], rs.at[4], right)
        got(buf.at[hr, bot], ss.at[2], rs.at[2])
        send(buf.at[hr, bot], buf.at[hr, bot], ss.at[5], rs.at[5], left)

    def ag_wait(buf, ss, rs, pos):
        if pos == 1:
            got(buf.at[hl, bot], ss.at[1], rs.at[1])
        if pos == 2:
            got(buf.at[hr, top], ss.at[3], rs.at[3])
        if pos == 3:
            got(buf.at[ho, top], ss.at[4], rs.at[4])
            got(buf.at[ho, bot], ss.at[5], rs.at[5])

    ag_two = lambda q: (n2.at[q], m_s.at[q], m_r.at[q])

    class Gathered:
        def __init__(self, part, halves, load, ss, rs, vs, vr):
            self.part, self.halves, self.load = part, halves, load
            self.sems = (ss, rs, vs, vr)

        def copy(self, i):
            low, high = self.halves
            at, rows, dev = ((h, low, right), (h, high, right), (h, high, left), (h, low, left),
                             (hl, low, right), (hr, high, left))[i]
            block = self.part(at, rows)
            return rc(block, block, self.sems[0].at[i], self.sems[1].at[i], dev)

        def arrive(self, i):
            low, high = self.halves
            at, rows = ((hl, low), (hl, high), (hr, high), (hr, low), (ho, low), (ho, high))[i]
            got(self.part(at, rows), self.sems[0].at[i], self.sems[1].at[i])

        def give(self, pos):
            block = self.part(order[pos], None)
            return rc(block, block, self.sems[2].at[pos], self.sems[3].at[pos], partner)

        def start(self):
            @pl.when(home)
            def _():
                loads[self.load].wait()
                for i in (0, 2, 1, 3):
                    self.copy(i).start()

        def forward(self):
            @pl.when(home)
            def _():
                self.arrive(0)
                self.copy(4).start()
                self.arrive(2)
                self.copy(5).start()

        def pull(self, pos):
            @pl.when(home)
            def _():
                for i in ((), (1,), (3,), (4, 5))[pos]:
                    self.arrive(i)
                self.give(pos).start()

        def take(self, pos):
            @pl.when(away)
            def _():
                self.give(pos).wait_recv()

        def drain(self):
            for i in range(6):
                self.copy(i).wait_send()
            for pos in range(4):
                self.give(pos).wait_send()

    w_qkv = Gathered(
        lambda at, rows: wq.at[at] if rows is None else wq.at[at, :, rows],
        (pl.ds(0, 512), pl.ds(512, 512)), 1, w_s, w_r, v_s, v_r,
    )
    w_out = Gathered(
        lambda at, rows: wo.at[at] if rows is None else wo.at[at, rows], (top, bot), 5, wo_s, wo_r, u_s, u_r
    )

    def qkv(q, pos):
        r = order[pos]
        for i in range(3):
            part = jnp.dot(nq[q], wq[r, i], preferred_element_type=F32)
            qs[q, r, :, i * 256:(i + 1) * 256] = part.astype(BF16)

        for of, oy, ox in PLANE:
            df, dy, dx = (f + of) % 2, (y + oy) % 2, (x + ox) % 4
            rc(
                qs.at[q, r, pl.ds((df * 8 + dy * 4 + dx) * 16, 16)], qr.at[q, r, book],
                a_s.at[q, r], a_r.at[q, r], (df, dy * 8 + dx * 2 + k, h),
            ).start()
        qr[q, r, book] = qs[q, r, pl.ds(pl.multiple_of(worker * 16, 16), 16), :]

    def attend(q, pos):
        r = order[pos]
        got(qr.at[q, r, pl.ds(0, 15)], a_s.at[q, r], a_r.at[q, r])

        def unit(n, carry):
            pair = n * 128
            take = lambda i: qr[
                q, r, :, :, pl.ds(pl.multiple_of(i * 256 + pair, 128), 128)
            ].reshape(256, 128)
            qq, kk, v = take(0), take(1), take(2)
            lane = lax.broadcasted_iota(jnp.int32, (256, 128), 1)
            halves = []
            for half in range(2):
                mine = (lane // 64) == half
                qh = jnp.where(mine, qq, jnp.zeros_like(qq))
                parts = []
                for rows, width in ((slice(0, 128), 128), (slice(128, 256), 256)):
                    s = lax.dot_general(
                        qh[rows], kk[:width], (((1,), (1,)), ((), ())), preferred_element_type=F32
                    )
                    s = s * 0.125 + bias[rows, :width]
                    e = jnp.exp(s - jnp.max(s, axis=-1, keepdims=True))
                    total = jnp.sum(e, axis=-1, keepdims=True)
                    o = jnp.dot(e.astype(BF16), v[:width], preferred_element_type=F32)
                    parts.append(o / total)
                halves.append(jnp.concatenate(parts, axis=0))
            o = jnp.where((lane // 64) == 0, halves[0], halves[1]).astype(BF16)
            att_s[q, r, :, :, pl.ds(pl.multiple_of(pair, 128), 128)] = o.reshape(16, 16, 128)
            return carry

        lax.fori_loop(0, 2, unit, 0)

        for of, oy, ox in PLANE:
            df, dy, dx = (f + of) % 2, (y + oy) % 2, (x + ox) % 4
            rc(
                att_s.at[q, r, dy * 8 + dx * 2 + df], att_r.at[q, r, pl.ds(worker * 16, 16)],
                b_s.at[q, r], b_r.at[q, r], (df, dy * 8 + dx * 2 + k, h),
            ).start()
        att_r[q, r, pl.ds(pl.multiple_of(worker * 16, 16), 16), :] = att_s[q, r, book]

    def out_proj(q):
        for src in order:
            got(att_r.at[q, src, pl.ds(0, 240)], b_s.at[q, src], b_r.at[q, src])

        def tile(n, carry):
            cols = pl.ds(pl.multiple_of(n * 256, 256), 256)
            total = x0[q, :, cols]
            for src in range(4):
                total = total + jnp.dot(att_r[q, src], wo[src, :, cols], preferred_element_type=F32)
            x0[q, :, cols] = total
            return carry

        lax.fori_loop(0, 4, tile, 0)
        norm_rows(q, n2.at[q, h], gain[1:2, :], x0, ())
        ag_start(*ag_two(q))

    def mine(q, pos, row0, rows, target):
        cols = pl.ds(pl.multiple_of(target * 256, 256), 256)
        value = jnp.dot(act[pl.ds((q * 4 + pos) * 256 + row0, rows), :], wd[:, cols], preferred_element_type=F32)
        if pos == 0:
            value = value + x0[q, pl.ds(row0, rows), cols]
        return value

    to_right = lambda q: owner(hr) if q else right
    to_left = lambda q: owner(hl) if q else left

    def last_copy(q, pos):
        r = order[pos]
        return rc(dos.at[q, pos], dor.at[q, r], e_s.at[q, pos], e_r.at[q, r], owner(h))

    def mlp(q, pos):
        r = order[pos]
        ss, rs = d_s.at[q, pos], d_r.at[q, r]
        ag_wait(*ag_two(q), pos)

        def tile(n, carry):
            cols = pl.ds(pl.multiple_of(n * 256, 256), 256)
            g = jnp.dot(n2[q, r], wgu[0, :, cols], preferred_element_type=F32)
            u = jnp.dot(n2[q, r], wgu[1, :, cols], preferred_element_type=F32)
            act[pl.ds((q * 4 + pos) * 256, 256), cols] = (g / (1.0 + jnp.exp(-g)) * u).astype(BF16)
            return carry

        lax.fori_loop(0, 4, tile, 0)
        ds2[q, pos] = mine(q, pos, 0, 256, ho).astype(BF16)
        send(ds2.at[q, pos, top], dfl.at[q, r], ss.at[0], rs.at[0], right)
        send(ds2.at[q, pos, bot], dfr.at[q, r], ss.at[1], rs.at[1], left)
        dsr[q, pos, bot, :] = mine(q, pos, 128, 128, hr).astype(BF16)
        send(dsr.at[q, pos, bot], drl.at[q, r, bot], ss.at[2], rs.at[2], to_right(q))
        dsl[q, pos, top, :] = mine(q, pos, 0, 128, hl).astype(BF16)
        send(dsl.at[q, pos, top], drr.at[q, r, top], ss.at[3], rs.at[3], to_left(q))
        if q == 0:
            oacc[q, pos] = mine(q, pos, 0, 256, h).reshape(4, 64, 256)
            return

        @pl.when(home)
        def _():
            oacc[q, pos] = mine(q, pos, 0, 256, h).reshape(4, 64, 256)

        @pl.when(away)
        def _():
            dos[q, pos] = mine(q, pos, 0, 256, h).astype(BF16)
            last_copy(q, pos).start()

    def pass_right(q, pos):
        r = order[pos]
        ss, rs = d_s.at[q, pos], d_r.at[q, r]
        got(dfl.at[q, r], ss.at[0], rs.at[0])
        dsr[q, pos, top, :] = (mine(q, pos, 0, 128, hr) + dfl[q, r].astype(F32)).astype(BF16)
        send(dsr.at[q, pos, top], drl.at[q, r, top], ss.at[4], rs.at[4], to_right(q))

    def pass_left(q, pos):
        r = order[pos]
        ss, rs = d_s.at[q, pos], d_r.at[q, r]
        got(dfr.at[q, r], ss.at[1], rs.at[1])
        dsl[q, pos, bot, :] = (mine(q, pos, 128, 128, hl) + dfr[q, r].astype(F32)).astype(BF16)
        send(dsl.at[q, pos, bot], drr.at[q, r, bot], ss.at[5], rs.at[5], to_left(q))

    def write(q, pos):
        return pltpu.make_async_copy(oacc.at[q, pos], out.at[order[pos], :, q], o_s.at[q, pos])

    def finish(q, pos):
        r = order[pos]
        for i, ref in (
            (2, drl.at[q, r, bot]), (3, drr.at[q, r, top]), (4, drl.at[q, r, top]), (5, drr.at[q, r, bot])
        ):
            got(ref, d_s.at[q, pos, i], d_r.at[q, r, i])
        gathered = drl[q, r].astype(F32) + drr[q, r].astype(F32)

        @pl.when(home)
        def _():
            oacc[q, pos] = oacc[q, pos] + gathered.reshape(4, 64, 256)
            write(q, pos).start()

        @pl.when(away)
        def _():
            if q == 0:
                dos[q, pos] = (oacc[q, pos].reshape(256, 256) + gathered).astype(BF16)
                last_copy(q, pos).start()
            else:
                last_copy(q, pos).wait_recv()
                oacc[q, pos] = (dor[q, r].astype(F32) + gathered).reshape(4, 64, 256)
                write(q, pos).start()

    def land(q, pos):
        @pl.when(away)
        def _():
            last_copy(q, pos).wait_recv()
            oacc[q, pos] = dor[q, order[pos]].astype(F32).reshape(4, 64, 256)
            write(q, pos).start()

    ids_out()
    temporal_out(0)
    w_qkv.start()
    row = lax.broadcasted_iota(jnp.int32, (256, 256), 0)
    col = lax.broadcasted_iota(jnp.int32, (256, 256), 1)
    bias[...] = jnp.where((row % 16 == col % 16) & (row // 16 >= col // 16), 0.0, -1e30)
    temporal_pass(0)
    temporal_out(1)
    ids_spread()
    loads[0].wait()
    temporal_in(0)
    temporal_pass(1)
    share_out((0, 1, 2))
    proj_far(0)
    proj_near(0)
    w_qkv.pull(0)
    proj_own(0)
    ready(0)
    ready(1)
    embed(0)
    proj_pass(0)
    temporal_in(1)
    proj_far(1)
    w_qkv.forward()
    w_qkv.pull(1)
    w_qkv.pull(2)
    embed(1)
    ready(2)
    norm_one(0)
    proj_near(1)
    x_in(0)
    w_qkv.take(0)
    qkv(0, 0)
    w_qkv.take(1)
    qkv(0, 1)
    w_qkv.take(2)
    qkv(0, 2)
    w_qkv.pull(3)
    w_qkv.take(3)
    qkv(0, 3)
    w_out.start()
    share_out((3, 4))
    proj_own(1)
    proj_pass(1)
    attend(0, 0)
    attend(0, 1)
    w_out.forward()
    attend(0, 2)
    attend(0, 3)
    norm_one(1)
    for pos in range(4):
        w_out.pull(pos)
    for pos in range(4):
        w_out.take(pos)
    out_proj(0)
    ready(3)
    ready(4)
    mlp(0, 0)
    x_in(1)
    together(1)
    qkv(1, 0)
    ag_forward(*ag_two(0))
    qkv(1, 1)
    qkv(1, 2)
    qkv(1, 3)
    mlp(0, 1)
    mlp(0, 2)
    pass_right(0, 1)
    pass_left(0, 2)
    attend(1, 0)
    attend(1, 1)
    mlp(0, 3)
    attend(1, 2)
    attend(1, 3)
    pass_right(0, 3)
    pass_left(0, 0)
    pass_right(0, 0)
    pass_left(0, 3)
    pass_right(0, 2)
    pass_left(0, 1)
    out_proj(1)
    mlp(1, 0)
    for pos in (1, 2, 0, 3):
        finish(0, pos)
    ag_forward(*ag_two(1))
    mlp(1, 1)
    mlp(1, 2)
    pass_right(1, 1)
    pass_left(1, 2)
    for pos in range(4):
        land(0, pos)
    mlp(1, 3)
    pass_right(1, 3)
    pass_left(1, 0)
    pass_right(1, 0)
    pass_left(1, 3)
    pass_right(1, 2)
    pass_left(1, 1)
    for pos in (1, 2, 0, 3):
        finish(1, pos)

    for s in sends:
        s.wait_send()
    for q in range(2):
        for r in range(4):
            block = qs.at[q, r, pl.ds(0, 240)]
            rc(block, block, a_s.at[q, r], a_r.at[q, r], right).wait_send()
            block = att_s.at[q, r, pl.ds(0, 15)]
            rc(block, block, b_s.at[q, r], b_r.at[q, r], right).wait_send()

    @pl.when(home)
    def _():
        w_qkv.drain()
        w_out.drain()
        for i in range(5):
            share(i).wait_send()

    @pl.when(away)
    def _():
        for q in range(2):
            own_copy(q).wait_send()
            for pos in range(4):
                last_copy(q, pos).wait_send()

    for q in range(2):
        for pos in range(4):
            write(q, pos).wait()


def body(temporal, frame_ids, proj_weight, embed_table, qkv_weight, out_weight, gate_up, down_weight, norm_gains):
    vm, dma = pltpu.VMEM, pltpu.SemaphoreType.DMA
    any_spec = pl.BlockSpec(memory_space=pl.ANY)
    result = pl.pallas_call(
        kernel,
        name="depth_layer",
        out_shape=jax.ShapeDtypeStruct((4, 4, 2, 64, 256), F32),
        in_specs=[any_spec] * 8 + [pl.BlockSpec(memory_space=pltpu.VMEM)],
        out_specs=any_spec,
        scratch_shapes=[
            vm((2, 16, 64, 1024), BF16), vm((1024, 1024), BF16), vm((4, 3, 1024, 256), BF16), vm((4, 256, 1024), BF16),
            vm((2, 1024, 1024), BF16), vm((1024, 1024), BF16), vm((2, 256, 1024), BF16),
            vm((1, 1024), BF16), vm((4, 128), jnp.int32), vm((4, 128), jnp.int32),
            vm((2, 256, 128), jnp.int32), vm((256, 2048), BF16),
            vm((2, 256, 1024), BF16), vm((2, 256, 1024), BF16), vm((2, 256, 1024), BF16),
            vm((2, 128, 1024), BF16), vm((2, 128, 1024), BF16), vm((2, 256, 1024), BF16), vm((2, 256, 1024), BF16),
            vm((2, 256, 1024), F32),
            vm((2, 256, 1024), BF16), vm((2, 256, 1024), BF16), vm((2, 256, 1024), BF16), vm((2, 4, 256, 768), BF16), vm((2, 4, 16, 16, 768), BF16),
            vm((2, 4, 16, 16, 256), BF16), vm((2, 4, 256, 256), BF16), vm((256, 256), F32), vm((2, 1024), F32),
            vm((2, 4, 256, 1024), BF16), vm((2048, 1024), BF16),
            vm((2, 4, 256, 256), BF16), vm((2, 4, 256, 256), BF16), vm((2, 4, 256, 256), BF16),
            vm((2, 4, 128, 256), BF16), vm((2, 4, 128, 256), BF16),
            vm((2, 4, 256, 256), BF16), vm((2, 4, 256, 256), BF16),
            vm((2, 4, 256, 256), BF16), vm((2, 4, 256, 256), BF16), vm((2, 4, 4, 64, 256), F32),
            dma((10,)), dma((1,)), dma((1,)), dma((2, 15)), dma((2, 16)), dma((6,)), dma((6,)), dma((2, 6)), dma((2, 6)),
            dma((6,)), dma((6,)), dma((4,)), dma((4,)), dma((4,)), dma((4,)), dma((5,)), dma((5,)), dma((2, 4)), dma((2, 4)),
            dma((2,)), dma((2,)), dma((2, 6)), dma((2, 6)), dma((2, 4)), dma((2, 4)), dma((2, 4)), dma((2, 4)),
            dma((2, 4, 6)), dma((2, 4, 6)), dma((2, 4)), pltpu.SemaphoreType.REGULAR((2,)),
        ],
        compiler_params=pltpu.CompilerParams(
            collective_id=0, has_side_effects=True, vmem_limit_bytes=67043328
        ),
    )(
        temporal.reshape(2, 64, 1024), frame_ids.reshape(4, 4, 128), embed_table, proj_weight, qkv_weight, out_weight, gate_up, down_weight, norm_gains
    )
    return result.reshape(1, 2048, 256)


def solution(mesh):
    placed = (
        P(("frames", "codebook"), "hidden"),
        P("frames", "codebook"),
        P("codebook", "hidden", None),
        P("codebook", None, None),
        P("codebook", None, None, "hidden"),
        P("codebook", "hidden", None),
        P("codebook", None, None, "hidden"),
        P("codebook", "hidden", None),
        P("codebook", None, None),
    )
    return jax.shard_map(
        body,
        mesh=mesh,
        in_specs=placed,
        out_specs=P("codebook", "frames", "hidden"),
        check_vma=False,
    )
```
